256 devices in a mesh: span: 32 (over z_hi, x, core), chord: 8 (over z_lo, y).
Axes of the slice: x: 4, y: 4, z: 8 (z_hi: 4, z_lo: 2; z = z_hi * 2 + z_lo), core: 2. Of those that a mesh axis runs over, the one named last changes fastest.
Arguments:
- flow_state: float32 [3, 1024, 64, 1024], P(None, 'span', None, 'chord'), may hold values from -6 to 6
- vel_span: bfloat16 [1024, 64, 1024], P('span', None, 'chord'), may hold values from -1 to 1
- vel_chord: bfloat16 [1024, 64, 1024], P('span', None, 'chord'), may hold values from -1 to 2.5
- viscosity: bfloat16 [1024, 64, 1024], P('span', None, 'chord'), may hold values from 0.0099487305 to 0.119628906
- mixing: float32 [3, 3], replicated, may hold values from -0.5 to 0.5
- te_index: int32 [1024], P('span'), may hold values from 0 to 1023
- band_response: float32 [64, 2, 64], replicated, may hold values from -0.75 to 0.75
- spectra: bfloat16 [1024, 64, 128], P('span', 'chord'), may hold values from -6 to 6
- offsets: int32 [16], replicated, may hold values from 0 to 63
- prior_gram_blocks: float32 [2, 64, 1024, 1024], P(None, 'chord', 'span'), may hold values from -6 to 6
Outputs:
- flow_next: float32 [3, 1024, 64, 1024], P(None, 'span', None, 'chord')
- gram_next: float32 [2, 64, 1024, 1024], P(None, 'chord', 'span')
The draws below stay inside these ranges and needn't reach their ends.
All inputs are finite; a program needn't handle non-finite values.
Results may differ from the reference program's by a relative error of at most 0.0025.
Values may be sent and summed in bfloat16 or wider, within the bound.
No kernel may reach another device: no remote copies, remote signals or barrier semaphores. Data moves between devices by JAX's collectives and lax.ppermute only.
A program may use at most 128 MiB of HBM per device.

```python
import math
import jax
import jax.numpy as jnp
from jax import lax

NN = 64
COMPS = 3
BANDS = 64
SLOTS = 64
SEGS = 16
NSPAN = 1024
NCHORD = 1024


def draw_flow_state(key, part):
    drawn_draw = jax.random.normal(key, (COMPS, NSPAN, NN, NCHORD), jnp.float32)
    result = jnp.clip(drawn_draw, -6.0, 6.0)
    return result.astype(jnp.float32)


def draw_vel_chord(key, part):
    speeds = jax.random.uniform(key, (NSPAN, NN, NCHORD), jnp.float32, minval=-1.0, maxval=1.0)
    return speeds.astype(jnp.bfloat16)


def set_ends(values, key, low, high):
    longest = values.shape.index(max(values.shape))
    spots = []
    for shift in (0, 1):
        where = [jax.random.randint(jax.random.fold_in(key, axis), (), 0, length) for axis, length in enumerate(values.shape)]
        where[longest] = (where[longest] + shift) % values.shape[longest]
        spots.append(tuple(where))
    return values.at[spots[0]].set(low).at[spots[1]].set(high)


def steps_of(own_key, shape, split, smallest, high):
    def one(position, shards_of):
        draws = jax.random.uniform(jax.random.fold_in(jax.random.fold_in(own_key, 6), position), (shards_of,), jnp.float32, smallest / len(split), high / len(split))
        return jnp.repeat(jnp.exp(draws), shape[position] // shards_of).reshape((-1,) + (1,) * (len(shape) - position - 1))

    level = one(*split[0])
    for cut in split[1:]:
        level = level * one(*cut)
    return level


def bell_draw(rng, shape, scale, bound, split=(), kind=jnp.bfloat16):
    level = steps_of(rng, shape, split, -0.22, 0.18) if split else 1.0
    array = jax.random.normal(rng, shape, jnp.float32) * scale * level
    return jnp.minimum(jnp.maximum(array, -bound), bound).astype(kind)


def setup_inputs(seed: int = 0) -> dict:
    seeds = jax.random.split(jax.random.key(seed), 11)
    return {
        "flow_state": draw_flow_state(jax.random.fold_in(seeds[10], 71), 0),
        "vel_span": jnp.clip(jax.random.uniform(seeds[1], (NSPAN, NN, NCHORD), jnp.float32, -1.0, 1.0) * steps_of(seeds[1], (NSPAN, NN, NCHORD), ((0, 32), (2, 8)), -0.4, 0.0), -1.0, 1.0).astype(jnp.bfloat16),
        "vel_chord": draw_vel_chord(jax.random.fold_in(seeds[10], 71), 0),
        "viscosity": jnp.clip(jnp.exp(math.log(0.119628906) - 2.48694955 * jax.random.uniform(seeds[3], (NSPAN, NN, NCHORD), jnp.float32) ** steps_of(seeds[3], (NSPAN, NN, NCHORD), ((0, 32), (2, 8)), -0.2, 0.2)), 0.0099487305, 0.119628906).astype(jnp.bfloat16),
        "mixing": jnp.clip(jax.random.uniform(seeds[4], (COMPS, COMPS), jnp.float32, -0.5, 0.5), -0.5, 0.5),
        "te_index": set_ends(jax.random.randint(seeds[5], (NSPAN,), 0, NCHORD), jax.random.fold_in(seeds[5], 1), 0, NCHORD - 1).astype(jnp.int32),
        "band_response": bell_draw(seeds[6], (NN, 2, BANDS), NN ** -0.5, 0.75, (), jnp.float32),
        "spectra": bell_draw(seeds[7], (NSPAN, BANDS, 2 * SLOTS), 1.0, 6.0, ((0, 32), (1, 8))),
        "offsets": set_ends(jax.random.randint(seeds[8], (SEGS,), 0, SLOTS), jax.random.fold_in(seeds[8], 1), 0, SLOTS - 1).astype(jnp.int32),
        "prior_gram_blocks": bell_draw(seeds[9], (2, BANDS, NSPAN, NSPAN), 1.0, 6.0, ((1, 8), (2, 32)), jnp.float32),
    }


first_coeffs = (0.75, -0.15, 1.0 / 60.0)
second_coeffs = (1.5, -0.15, 1.0 / 90.0)
centre_coeff = -49.0 / 18.0
time_step = 0.6
decay_factor = 0.9


def window(padded, axis_pos, length, offset):
    return lax.slice_in_dim(padded, 3 + offset, 3 + offset + length, axis=axis_pos)


def first_diff(padded, axis_pos, length):
    result = jnp.zeros_like(window(padded, axis_pos, length, 0))
    for reach in (1, 2, 3):
        result = result + first_coeffs[reach - 1] * (window(padded, axis_pos, length, reach) - window(padded, axis_pos, length, -reach))
    return result


def second_diff(padded, axis_pos, length):
    result = centre_coeff * window(padded, axis_pos, length, 0)
    for reach in (1, 2, 3):
        result = result + second_coeffs[reach - 1] * (window(padded, axis_pos, length, reach) + window(padded, axis_pos, length, -reach))
    return result


def tendency(flow, speed_span, speed_chord, visc, mixing):
    span_len = flow.shape[1]
    normal_len = flow.shape[2]
    chord_len = flow.shape[3]
    span_padding = jnp.concatenate([flow[:, span_len - 3:], flow, flow[:, :3]], axis=1)
    chord_pad = jnp.pad(flow, ((0, 0), (0, 0), (0, 0), (3, 3)))
    normal_pad = jnp.pad(flow, ((0, 0), (0, 0), (3, 3), (0, 0)))
    diffusion = second_diff(span_padding, 1, span_len) + second_diff(chord_pad, 3, chord_len) + second_diff(normal_pad, 2, normal_len)
    cross_coupling = jnp.einsum('qe,esnc->qsnc', mixing, flow, precision=lax.Precision.HIGHEST)
    return (-speed_span * first_diff(span_padding, 1, span_len) - speed_chord * first_diff(chord_pad, 3, chord_len)
            + visc * diffusion + cross_coupling)


def segment_weights(seg_count):
    ramp = (lax.iota(jnp.int32, seg_count + 1) + 1).astype(jnp.float32) / seg_count
    ramp = jnp.minimum(ramp, jnp.float32(1.0))
    return jnp.concatenate([ramp, ramp])


def reference(flow_state, vel_span, vel_chord, viscosity, mixing, te_index, band_response, spectra, offsets, prior_gram_blocks):
    speed_span = vel_span.astype(jnp.float32)
    speed_chord = vel_chord.astype(jnp.float32)
    visc = viscosity.astype(jnp.float32)
    section_one = flow_state + time_step * tendency(flow_state, speed_span, speed_chord, visc, mixing)
    flow_next = 0.5 * (flow_state + section_one + time_step * tendency(section_one, speed_span, speed_chord, visc, mixing))
    surface = flow_next[0]
    stations = surface.shape[0]
    index_block = jnp.broadcast_to(te_index.astype(jnp.int32)[:, None, None], (stations, surface.shape[1], 1))
    normal_profile = jnp.take_along_axis(surface, index_block, axis=2)[:, :, 0]
    band_magnitude = jnp.einsum('vg,gkl->vlk', normal_profile, band_response, precision=lax.Precision.HIGHEST).astype(jnp.bfloat16)
    stored = spectra.reshape(stations, BANDS, 2, SLOTS)
    picked = jnp.take(stored, offsets.astype(jnp.int32), axis=3)
    segments = jnp.concatenate([picked, band_magnitude[:, :, :, None]], axis=3)
    flat = segments.astype(jnp.float32).reshape(stations, BANDS, 2 * (SEGS + 1))
    turned = jnp.concatenate([segments[:, :, 1], -segments[:, :, 0]], axis=2).astype(jnp.float32)
    weights = segment_weights(SEGS)
    real_part = jnp.einsum('ibk,jbk->bij', flat * weights, flat, precision=lax.Precision.HIGHEST)
    imag_part = jnp.einsum('ibk,jbk->bij', turned * weights, flat, precision=lax.Precision.HIGHEST)
    gram_next = decay_factor * prior_gram_blocks + jnp.stack([real_part, imag_part])
    return flow_next, gram_next
```

```python
import functools

import jax
import jax.numpy as jnp
import ml_dtypes
import numpy as np
from jax import lax
from jax.experimental import pallas as pl
from jax.experimental.pallas import tpu as pltpu
from jax.sharding import PartitionSpec as P

FIRST = (45, -9, 1)
SECOND = (270, -27, 2)
CENTRE = -490
TIME_STEP = 0.6
DECAY = 0.9
F32 = jnp.float32
BF16 = jnp.bfloat16
LANES = 128


def chord_matrices():
    inner = np.zeros((LANES, 2 * LANES), np.float32)
    halo = np.zeros((8, 2 * LANES), np.float32)

    def row(cell):
        if cell < 0:
            return halo, cell + 3
        if cell >= LANES:
            return halo, cell - LANES + 3
        return inner, cell

    for cell in range(LANES):
        inner[cell, LANES + cell] += CENTRE
        for reach in (1, 2, 3):
            for sign in (1, -1):
                table, index = row(cell + sign * reach)
                table[index, cell] += sign * FIRST[reach - 1]
                table[index, LANES + cell] += SECOND[reach - 1]
    edges = np.zeros((8, LANES), np.float32)
    for k in range(3):
        edges[k, LANES - 3 + k] = 1
        edges[3 + k, k] = 1
    bf = ml_dtypes.bfloat16
    return (
        np.concatenate([inner, inner]).astype(bf),
        halo.astype(bf),
        np.concatenate([edges, edges], axis=1).astype(bf),
    )


def split_two(x):
    high = x.astype(BF16)
    low = (x - high.astype(F32)).astype(BF16)
    return jnp.concatenate([high, low], axis=1)


def nt_dot(a, b):
    return lax.dot_general(a, b, (((1,), (1,)), ((), ())), preferred_element_type=F32)


def edges_kernel(flow_ref, pick_ref, right_ref, left_ref, *, pairs):
    quantities = flow_ref.shape[0]
    for q in range(quantities):
        for p in range(pairs):
            slab = flow_ref[q, 2 * p : 2 * p + 2].reshape(LANES, LANES)
            got = nt_dot(pick_ref[...], split_two(slab))
            for k in range(3):
                right_ref[0, k, q * pairs + p, :] = got[k, :]
                left_ref[0, k, q * pairs + p, :] = got[3 + k, :]


def section_kernel(
    *refs, quantities, second, profile, carried
):
    refs = list(refs)
    take = refs.pop
    state_hbm = take(0)
    span_low, span_high, chord_low, chord_high = (take(0) for _ in range(4))
    vs_hbm, vc_hbm, nu_hbm = (take(0) for _ in range(3))
    mix = take(0)
    inner_ref, halo_ref, pick_ref = (take(0) for _ in range(3))
    if second:
        flow_hbm = take(0)
    if profile:
        te_ref, band_ref = take(0), take(0)
    if carried:
        take(0)
    out_hbm = take(0)
    if not second:
        low_out, high_out, right_out, left_out = (take(0) for _ in range(4))
    if profile:
        amp_out = take(0)
    wide, result, chord, halos, vs, vc, nu, in_sem, out_sem = (take(0) for _ in range(9))
    if second:
        before, before_sem = take(0), take(0)
    if profile:
        columns, amps = take(0), take(0)

    count = len(quantities)
    first_q = quantities[0]
    stations, normal = vs.shape[0], vs.shape[1]
    chunks, pairs = 4, stations // 2
    per = stations // chunks

    def copies(c):
        rows = pl.ds(per * c, per)
        todo = [
            pltpu.make_async_copy(
                state_hbm.at[:, rows],
                wide.at[:, pl.ds(3 + per * c, per), pl.ds(8, normal), :],
                in_sem.at[0, c],
            ),
            pltpu.make_async_copy(vs_hbm.at[rows], vs.at[rows], in_sem.at[1, c]),
            pltpu.make_async_copy(vc_hbm.at[rows], vc.at[rows], in_sem.at[2, c]),
            pltpu.make_async_copy(nu_hbm.at[rows], nu.at[rows], in_sem.at[3, c]),
        ]
        if second:
            todo.append(
                pltpu.make_async_copy(
                    flow_hbm.at[pl.ds(first_q, count), rows], before.at[:, rows], before_sem.at[c]
                )
            )
        return todo

    for c in range(chunks):
        for copy in copies(c):
            copy.start()

    nothing = jnp.zeros(wide.shape[:2] + (8, LANES), F32)
    wide[:, :, 0:8, :] = nothing
    wide[:, :, 8 + normal : 16 + normal, :] = nothing
    wide[:, 0:3, 8 : 8 + normal, :] = span_low[...].astype(F32)
    wide[:, 3 + stations : 6 + stations, 8 : 8 + normal, :] = span_high[...].astype(F32)
    slabs = chord_low.shape[1]
    for k in range(3):
        halos[pl.ds(k, slabs, stride=8), :] = chord_low[k]
        halos[pl.ds(3 + k, slabs, stride=8), :] = chord_high[k]
    for k in (6, 7):
        halos[pl.ds(k, slabs, stride=8), :] = jnp.zeros((slabs, LANES), F32)
    if profile:
        columns[...] = jnp.zeros(columns.shape, F32)

    def matmuls(p):
        slot = p % 2
        for local, q in enumerate(quantities):
            slab = wide[q, pl.ds(3 + 2 * p, 2), 8 : 8 + normal, :].reshape(LANES, LANES)
            start = pl.multiple_of((q * pairs + p) * 8, 8)
            halo = halos[pl.ds(start, 8), :].T.astype(BF16)
            chord[slot, local] = jnp.dot(
                split_two(slab), inner_ref[...], preferred_element_type=F32
            ) + jnp.dot(halo, halo_ref[...], preferred_element_type=F32)

    def edge_cells(p):
        for q in quantities:
            slab = result[q - first_q, pl.ds(2 * p, 2)].reshape(LANES, LANES)
            got = nt_dot(pick_ref[...], split_two(slab))
            for k in range(3):
                right_out[k, pl.ds(q * pairs + p, 1), :] = got[k : k + 1, :]
                left_out[k, pl.ds(q * pairs + p, 1), :] = got[3 + k : 4 + k, :]

    scale = 0.5 if second else 1.0
    couple = [
        [
            scale * ((1.0 if q == e else 0.0) + TIME_STEP * mix[q, e])
            for e in range(wide.shape[0])
        ]
        for q in quantities
    ]
    lane = lax.broadcasted_iota(jnp.int32, (16, LANES), 1)

    def body(p, carry):
        matmuls(jnp.minimum(p + 1, pairs - 1))
        slot = p % 2
        for half in range(2):
            s = 2 * p + half
            for tile in range(normal // 16):
                rows = slice(16 * tile, 16 * tile + 16)
                a = vs[s, rows, :].astype(F32) * (-scale * TIME_STEP / 60)
                b = vc[s, rows, :].astype(F32) * (-scale * TIME_STEP / 60)
                g = nu[s, rows, :].astype(F32) * (scale * TIME_STEP / 180)
                centre = [
                    wide[e, 3 + s, 8 + 16 * tile : 24 + 16 * tile, :]
                    for e in range(wide.shape[0])
                ]
                for local, q in enumerate(quantities):

                    def at(ds, dn):
                        low = 8 + 16 * tile + dn
                        return wide[q, 3 + s + ds, low : low + 16, :]

                    first = None
                    both = None
                    for reach in (1, 2, 3):
                        up, down = at(reach, 0), at(-reach, 0)
                        diff = up - down
                        total = (up + down) + (at(0, reach) + at(0, -reach))
                        if FIRST[reach - 1] != 1:
                            diff = diff * float(FIRST[reach - 1])
                        total = total * float(SECOND[reach - 1])
                        first = diff if first is None else first + diff
                        both = total if both is None else both + total
                    crow = slice(64 * half + 16 * tile, 64 * half + 16 * tile + 16)
                    chord_first = chord[slot, local, crow, 0:LANES]
                    chord_second = chord[slot, local, crow, LANES : 2 * LANES]
                    both = both + (centre[q] * float(2 * CENTRE) + chord_second)
                    value = a * first + b * chord_first + g * both
                    for e in range(wide.shape[0]):
                        value = value + couple[local][e] * centre[e]
                    if second:
                        value = value + 0.5 * before[local, s, rows, :]
                    result[local, s, rows, :] = value
                    if profile:
                        hit = jnp.where(lane == te_ref[s], value, 0.0)
                        column = jnp.sum(hit, axis=1, keepdims=True)
                        columns[rows, :] += jnp.where(lane == s, column, 0.0)
        both_stations = pl.ds(2 * p, 2)
        pltpu.make_async_copy(
            result.at[:, both_stations],
            out_hbm.at[pl.ds(first_q, count), both_stations],
            out_sem.at[p],
        ).start()
        if not second:
            edge_cells(p)
        return carry

    def arrive(c):
        for copy in copies(c):
            copy.wait()

    arrive(0)
    matmuls(0)
    for c in range(chunks):
        if c + 1 < chunks:
            arrive(c + 1)
        lax.fori_loop(c * pairs // chunks, (c + 1) * pairs // chunks, body, 0)

    if not second:
        low_out[...] = result[:, 0:3].astype(BF16)
        high_out[...] = result[:, stations - 3 : stations].astype(BF16)
    if profile:
        amp = lax.dot_general(
            columns[...].T,
            band_ref[...],
            (((1,), (0,)), ((), ())),
            precision=lax.Precision.HIGHEST,
            preferred_element_type=F32,
        )
        amps[...] = amp[:stations].astype(BF16).astype(F32)
        lane4 = lax.broadcasted_iota(jnp.int32, (4, LANES), 1) // 16
        pieces = [jnp.zeros((4, LANES), F32) for _ in range(8)]
        for u in range(8):
            some = amps[pl.ds(u, 4, stride=8), :]
            for j in range(8):
                shift = (16 * (u - j)) % LANES
                moved = pltpu.roll(some, shift, 1) if shift else some
                pieces[j] = jnp.where(lane4 == u, moved, pieces[j])
        for j in range(8):
            amp_out[j] = pieces[j]

    def drain(p, carry):
        both_stations = pl.ds(2 * p, 2)
        pltpu.make_async_copy(
            result.at[:, both_stations],
            out_hbm.at[pl.ds(first_q, count), both_stations],
            out_sem.at[p],
        ).wait()
        return carry

    lax.fori_loop(0, pairs, drain, 0)


def section(
    state,
    halos,
    fields,
    mixing,
    tables,
    quantities,
    flow=None,
    te_local=None,
    band_table=None,
    onto=None,
):
    all_q, stations, normal, _ = state.shape
    second = flow is not None
    profile = te_local is not None
    carried = onto is not None
    count = len(quantities)
    pairs = stations // 2
    hbm = pl.BlockSpec(memory_space=pl.ANY)
    vmem = pl.BlockSpec(memory_space=pltpu.VMEM)
    smem = pl.BlockSpec(memory_space=pltpu.SMEM)
    args = [state, *halos, *fields, mixing, *tables]
    specs = [hbm] + [vmem] * 4 + [hbm] * 3 + [smem] + [vmem] * 3
    if second:
        args.append(flow)
        specs.append(hbm)
    if profile:
        args += [te_local, band_table]
        specs += [smem, vmem]
    aliases = {}
    if carried:
        aliases = {len(args): 0}
        args.append(onto)
        specs.append(hbm)
    shapes = [jax.ShapeDtypeStruct(state.shape, F32)]
    outs = [hbm]
    if not second:
        shapes += [jax.ShapeDtypeStruct((all_q, 3, normal, LANES), BF16)] * 2
        shapes += [jax.ShapeDtypeStruct((3, all_q * pairs, LANES), F32)] * 2
        outs += [vmem] * 4
    if profile:
        shapes.append(jax.ShapeDtypeStruct((8, 4, LANES), F32))
        outs.append(vmem)
    scratch = [
        pltpu.VMEM((all_q, stations + 6, normal + 16, LANES), F32),
        pltpu.VMEM((count, stations, normal, LANES), F32),
        pltpu.VMEM((2, count, LANES, 2 * LANES), F32),
        pltpu.VMEM((all_q * pairs * 8, LANES), F32),
        pltpu.VMEM((stations, normal, LANES), BF16),
        pltpu.VMEM((stations, normal, LANES), BF16),
        pltpu.VMEM((stations, normal, LANES), BF16),
        pltpu.SemaphoreType.DMA((4, 4)),
        pltpu.SemaphoreType.DMA((pairs,)),
    ]
    if second:
        scratch += [
            pltpu.VMEM((count, stations, normal, LANES), F32),
            pltpu.SemaphoreType.DMA((4,)),
        ]
    if profile:
        scratch += [pltpu.VMEM((normal, LANES), F32), pltpu.VMEM((stations, LANES), F32)]
    return pl.pallas_call(
        functools.partial(
            section_kernel,
            quantities=quantities,
            second=second,
            profile=profile,
            carried=carried,
        ),
        out_shape=tuple(shapes),
        in_specs=specs,
        out_specs=tuple(outs),
        scratch_shapes=scratch,
        input_output_aliases=aliases,
        compiler_params=pltpu.CompilerParams(vmem_limit_bytes=40 << 20),
        cost_estimate=pl.CostEstimate(
            flops=20000000 * count, transcendentals=0, bytes_accessed=5000000 * count
        ),
        name="section_" + ("two" if second else "one") + "_" + "".join(map(str, quantities)),
    )(*args)


def stored_kernel(prior_ref, left_ref, all_ref, out_ref, *, bands):
    step = pl.program_id(1)
    stations = left_ref.shape[2]
    lane_band = lax.broadcasted_iota(jnp.int32, (stations, 2 * LANES), 1) // 32
    parts = []
    for level in range(2):
        for b in range(bands):
            parts.append(jnp.where(lane_band == step * bands + b, left_ref[0, level], 0.0))
    left = jnp.concatenate(parts).astype(BF16)
    got = nt_dot(left, all_ref[...])
    half = bands * stations
    total = got[:half] + got[half:]
    out_ref[0] = DECAY * prior_ref[0] + total.reshape(bands, stations, -1)


def amplitude_kernel(known_ref, amp_ref, where_ref, rep_ref, out_ref, spread, left, *, bands):
    kind, step = pl.program_id(0), pl.program_id(1)
    stations = left.shape[1]
    rows = amp_ref.shape[0]

    @pl.when(jnp.logical_and(kind == 0, step == 0))
    def _():
        lane = lax.broadcasted_iota(jnp.int32, (8, LANES), 1) // 16
        own = lane == lax.broadcasted_iota(jnp.int32, (8, LANES), 0)
        for r in range(0, rows, 2):
            two = [
                jnp.where(own, jnp.broadcast_to(amp_ref[r + d : r + d + 1, :], (8, LANES)), 0.0)
                for d in range(2)
            ]
            spread[8 * r : 8 * r + 16, :] = jnp.concatenate(two).astype(BF16)
        first = pl.multiple_of(where_ref[0] * stations, stations)
        mine = spread[pl.ds(first, stations), :]
        for c in range(2):
            left[c] = jnp.dot(mine, rep_ref[c], preferred_element_type=F32)

    lane_band = lax.broadcasted_iota(jnp.int32, (stations, LANES), 1) % 8
    parts = [
        jnp.where(lane_band == step * bands + b, left[kind], 0.0) for b in range(bands)
    ]
    got = nt_dot(jnp.concatenate(parts).astype(BF16), spread[...])
    out_ref[0] = known_ref[0] + got.reshape(bands, stations, -1)


def amplitude_tables():
    index = np.arange(LANES)
    same = (index[:, None] % 16 == index[None, :] % 16).astype(np.float32)
    other = (index[:, None] % 8 == index[None, :] % 8) & (
        (index[:, None] % 16) // 8 != (index[None, :] % 16) // 8
    )
    sign = np.where((index % 16) // 8 == 0, 1.0, -1.0)
    return np.stack([same, other * sign[None, :]]).astype(ml_dtypes.bfloat16)


def shards(
    flow_state,
    vel_span,
    vel_chord,
    viscosity,
    mixing,
    te_index,
    band_response,
    spectra,
    offsets,
    prior_gram_blocks,
):
    quantities, stations, normal, cells = flow_state.shape
    bands, slots = spectra.shape[1], spectra.shape[2] // 2
    segs = offsets.shape[0]
    pairs = stations // 2
    span_n, chord_n = lax.axis_size("span"), lax.axis_size("chord")
    span_pos, chord_pos = lax.axis_index("span"), lax.axis_index("chord")
    tables = chord_matrices()
    fields = (vel_span, vel_chord, viscosity)

    def exchange(low, high, right, left):
        up = [(i, (i + 1) % span_n) for i in range(span_n)]
        down = [(b, a) for a, b in up]
        forward = [(i, i + 1) for i in range(chord_n - 1)]
        backward = [(b, a) for a, b in forward]
        return (
            lax.ppermute(high, "span", up),
            lax.ppermute(low, "span", down),
            lax.ppermute(right, "chord", forward),
            lax.ppermute(left, "chord", backward),
        )

    blocks = 8
    per = stations // blocks
    right, left = pl.pallas_call(
        functools.partial(edges_kernel, pairs=per // 2),
        grid=(blocks,),
        out_shape=(jax.ShapeDtypeStruct((blocks, 3, quantities * per // 2, LANES), F32),) * 2,
        in_specs=[
            pl.BlockSpec((quantities, per, normal, cells), lambda i: (0, i, 0, 0)),
            pl.BlockSpec(tables[2].shape, lambda i: (0, 0)),
        ],
        out_specs=(
            pl.BlockSpec((1, 3, quantities * per // 2, LANES), lambda i: (i, 0, 0, 0)),
        )
        * 2,
        name="edges",
    )(flow_state, tables[2])

    def slab_order(x):
        x = x.reshape(blocks, 3, quantities, per // 2, LANES)
        return x.transpose(1, 2, 0, 3, 4).reshape(3, quantities * pairs, LANES)

    halos = exchange(
        flow_state[:, :3].astype(BF16),
        flow_state[:, stations - 3 :].astype(BF16),
        slab_order(right),
        slab_order(left),
    )

    rows = lax.broadcasted_iota(jnp.int32, (2 * slots, 2 * segs), 0)
    cols = lax.broadcasted_iota(jnp.int32, (2 * slots, 2 * segs), 1)
    wanted = jnp.concatenate([offsets, offsets + slots])
    choose = (rows == wanted[None, :]).astype(BF16)
    picked = jnp.dot(
        spectra.reshape(stations * bands, 2 * slots), choose, preferred_element_type=F32
    )
    packed = picked.astype(BF16).reshape(stations, bands * 2 * segs)
    every = lax.all_to_all(
        jnp.broadcast_to(packed[None], (span_n,) + packed.shape), "span", 0, 0, tiled=True
    ).reshape(span_n * stations, bands * 2 * segs)
    ramp = (jnp.arange(segs, dtype=jnp.int32) + 1).astype(F32) / segs
    quad = packed.astype(F32).reshape(stations, bands, 2, segs) * ramp
    turned = jnp.stack([quad[:, :, 1], -quad[:, :, 0]], axis=2)
    lefts = jnp.stack([quad, turned]).reshape(2, stations, bands * 2 * segs)
    lefts_high = lefts.astype(BF16).astype(F32)
    lefts = jnp.stack([lefts_high, lefts - lefts_high], axis=1)

    section_one, low, high, right, left = section(
        flow_state, halos, fields, mixing, tables, (0, 1, 2)
    )
    halos = exchange(low, high, right, left)

    group = 4
    gram_block = pl.BlockSpec(
        (1, group, stations, span_n * stations), lambda c, g: (c, g, 0, 0)
    )
    known = pl.pallas_call(
        functools.partial(stored_kernel, bands=group),
        grid=(2, bands // group),
        out_shape=jax.ShapeDtypeStruct(prior_gram_blocks.shape, F32),
        in_specs=[
            gram_block,
            pl.BlockSpec((1, 2, stations, bands * 2 * segs), lambda c, g: (c, 0, 0, 0)),
            pl.BlockSpec((span_n * stations, bands * 2 * segs), lambda c, g: (0, 0)),
        ],
        out_specs=gram_block,
        name="gram_stored",
        cost_estimate=pl.CostEstimate(
            flops=20000000, transcendentals=0, bytes_accessed=5000000
        ),
    )(prior_gram_blocks, lefts, every)

    te_local = te_index - chord_pos * cells
    band_table = band_response.reshape(normal, 2, chord_n, bands).transpose(0, 2, 1, 3)
    band_table = band_table.reshape(normal, chord_n * 2 * bands)
    flow_next, amps = section(
        section_one,
        halos,
        fields,
        mixing,
        tables,
        (0,),
        flow=flow_state,
        te_local=te_local,
        band_table=band_table,
    )
    amps = jnp.broadcast_to(amps.astype(BF16)[None], (span_n,) + amps.shape)
    amps = lax.all_to_all(
        amps.reshape((span_n * chord_n,) + amps.shape[2:]), ("span", "chord"), 0, 0, tiled=True
    )
    (flow_next,) = section(
        section_one,
        halos,
        fields,
        mixing,
        tables,
        (1, 2),
        flow=flow_state,
        onto=flow_next,
    )
    amps = jnp.sum(amps.reshape((span_n, chord_n) + amps.shape[1:]).astype(F32), axis=1)
    amps = amps.reshape(span_n * 4, LANES)
    gram_next = pl.pallas_call(
        functools.partial(amplitude_kernel, bands=group),
        grid=(2, bands // group),
        out_shape=jax.ShapeDtypeStruct(prior_gram_blocks.shape, F32),
        in_specs=[
            gram_block,
            pl.BlockSpec(amps.shape, lambda c, g: (0, 0)),
            pl.BlockSpec(memory_space=pltpu.SMEM),
            pl.BlockSpec((2, LANES, LANES), lambda c, g: (0, 0, 0)),
        ],
        out_specs=gram_block,
        scratch_shapes=[
            pltpu.VMEM((span_n * stations, LANES), BF16),
            pltpu.VMEM((2, stations, LANES), F32),
        ],
        name="gram_amplitudes",
    )(known, amps, span_pos.reshape(1), amplitude_tables())
    return (flow_next, gram_next)


def solution(mesh):
    return jax.shard_map(
        shards,
        mesh=mesh,
        in_specs=(
            P(None, "span", None, "chord"),
            P("span", None, "chord"),
            P("span", None, "chord"),
            P("span", None, "chord"),
            P(),
            P("span"),
            P(),
            P("span", "chord", None),
            P(),
            P(None, "chord", "span", None),
        ),
        out_specs=(P(None, "span", None, "chord"), P(None, "chord", "span", None)),
        check_vma=False,
    )
```

```python
import functools

import jax
import jax.numpy as jnp
import ml_dtypes
import numpy as np
from jax import lax
from jax.experimental import pallas as pl
from jax.experimental.pallas import tpu as pltpu
from jax.sharding import PartitionSpec as P

FIRST = (45, -9, 1)
SECOND = (270, -27, 2)
CENTRE = -490
TIME_STEP = 0.6
DECAY = 0.9
F32 = jnp.float32
BF16 = jnp.bfloat16
LANES = 128


def chord_matrices():
    inner = np.zeros((LANES, 2 * LANES), np.float32)
    outer = np.zeros((LANES, 2 * LANES), np.float32)

    def row(cell):
        if cell < 0:
            return outer, cell + 3
        if cell >= LANES:
            return outer, cell - LANES + 3
        return inner, cell

    for cell in range(LANES):
        inner[cell, LANES + cell] += CENTRE
        for reach in (1, 2, 3):
            for sign in (1, -1):
                table, index = row(cell + sign * reach)
                table[index, cell] += sign * FIRST[reach - 1]
                table[index, LANES + cell] += SECOND[reach - 1]
    return np.concatenate([inner, inner, outer]).astype(ml_dtypes.bfloat16)


def nt_dot(a, b):
    return lax.dot_general(a, b, (((1,), (1,)), ((), ())), preferred_element_type=F32)


def fine_dot(a, b):
    def pieces(x):
        one = x.astype(BF16)
        x = x - one.astype(F32)
        two = x.astype(BF16)
        return one, two, (x - two.astype(F32)).astype(BF16)

    left, right = pieces(a), pieces(b)
    total = None
    for i, j in ((2, 0), (0, 2), (1, 1), (1, 0), (0, 1), (0, 0)):
        part = jnp.dot(left[i], right[j], preferred_element_type=F32)
        total = part if total is None else total + part
    return total


def edge_lanes(shape):
    return lax.div(lax.broadcasted_iota(jnp.int32, shape, len(shape) - 1), 8)


def edges_kernel(flow_ref, cells_ref, low_ref, high_ref):
    stations, normal = flow_ref.shape[1:3]
    lane = edge_lanes((16, LANES))
    for half in range(stations // 16):
        for tile in range(normal // 16):
            rows = slice(16 * tile, 16 * tile + 16)
            packed = jnp.zeros((16, LANES), F32)
            for s in range(16):
                moved = pltpu.roll(flow_ref[0, 16 * half + s, rows, :], (3 + 8 * s) % LANES, 1)
                packed = jnp.where(lane == s, moved, packed)
            cells_ref[0, half, rows, :] = packed.astype(BF16)
    low_ref[0] = flow_ref[0, 0:3].astype(BF16)
    high_ref[0] = flow_ref[0, stations - 3 : stations].astype(BF16)


def section_kernel(*refs, second):
    take = list(refs).pop
    refs = list(refs)
    take = refs.pop
    state_hbm = take(0)
    span_low, span_high, chord_low, chord_high = (take(0) for _ in range(4))
    vs_hbm, vc_hbm, nu_hbm = (take(0) for _ in range(3))
    mix, table_ref = take(0), take(0)
    if second:
        flow_hbm, te_ref, band_ref = (take(0) for _ in range(3))
    out_hbm = take(0)
    if second:
        amp_out = take(0)
    else:
        low_out, high_out, cells_out = (take(0) for _ in range(3))
    wide, result, chord, halos, cells, vs, vc, nu, in_sem, out_sem = (take(0) for _ in range(10))
    if second:
        before, before_sem, columns, amps = (take(0) for _ in range(4))

    count, stations, normal = wide.shape[0], vs.shape[0], vs.shape[1]
    chunks, pairs = 4, stations // 2
    per = stations // chunks

    def copies(c):
        rows = pl.ds(per * c, per)
        todo = [
            pltpu.make_async_copy(
                state_hbm.at[:, rows],
                wide.at[:, pl.ds(3 + per * c, per), pl.ds(8, normal), :],
                in_sem.at[0, c],
            ),
            pltpu.make_async_copy(vs_hbm.at[rows], vs.at[rows], in_sem.at[1, c]),
            pltpu.make_async_copy(vc_hbm.at[rows], vc.at[rows], in_sem.at[2, c]),
            pltpu.make_async_copy(nu_hbm.at[rows], nu.at[rows], in_sem.at[3, c]),
        ]
        if second:
            todo.append(
                pltpu.make_async_copy(flow_hbm.at[:, rows], before.at[:, rows], before_sem.at[c])
            )
        return todo

    for c in range(chunks):
        for copy in copies(c):
            copy.start()

    nothing = jnp.zeros((count, stations, 8, LANES), F32)
    wide[:, 3 : 3 + stations, 0:8, :] = nothing
    wide[:, 3 : 3 + stations, 8 + normal : 16 + normal, :] = nothing
    wide[:, 0:3, 8 : 8 + normal, :] = span_low[...].astype(F32)
    wide[:, 3 + stations : 6 + stations, 8 : 8 + normal, :] = span_high[...].astype(F32)
    place = lax.rem(lax.broadcasted_iota(jnp.int32, (normal, LANES), 1), 8)
    for q in range(count):
        for half in range(stations // 16):
            near = jnp.where(
                place < 3, chord_low[q, half].astype(F32), chord_high[q, half].astype(F32)
            )
            halos[q, half] = jnp.where(place < 6, near, 0.0)
    if second:
        columns[...] = jnp.zeros(columns.shape, F32)

    def matmuls(p):
        slot, half = lax.rem(p, 2), lax.div(p, 8)
        parts = []
        for q in range(count):
            for d in range(2):
                slab = wide[q, 3 + 2 * p + d, 8 : 8 + normal, :]
                high = slab.astype(BF16)
                low = (slab - high.astype(F32)).astype(BF16)
                shift = lax.rem(LANES - 8 * lax.rem(2 * p + d, 16), LANES)
                beyond = pltpu.roll(halos[q, half], shift, 1).astype(BF16)
                parts.append(jnp.concatenate([high, low, beyond], axis=1))
        chord[slot] = jnp.dot(
            jnp.concatenate(parts), table_ref[...], preferred_element_type=F32
        )

    scale = 0.5 if second else 1.0
    couple = [
        [scale * ((1.0 if q == e else 0.0) + TIME_STEP * mix[q, e]) for e in range(count)]
        for q in range(count)
    ]
    ROWS = 16
    lane = lax.broadcasted_iota(jnp.int32, (ROWS, LANES), 1)

    def body(p, carry):
        matmuls(jnp.minimum(p + 1, pairs - 1))
        slot = lax.rem(p, 2)
        for half in range(2):
            s = 2 * p + half
            for tile in range(normal // ROWS):
                rows = slice(ROWS * tile, ROWS * tile + ROWS)
                a = vs[s, rows, :].astype(F32) * (-scale * TIME_STEP / 60)
                b = vc[s, rows, :].astype(F32) * (-scale * TIME_STEP / 60)
                g = nu[s, rows, :].astype(F32) * (scale * TIME_STEP / 180)
                centre = [
                    wide[e, 3 + s, 8 + ROWS * tile : 8 + ROWS * tile + ROWS, :]
                    for e in range(count)
                ]
                for q in range(count):

                    def at(ds, dn):
                        low = 8 + ROWS * tile + dn
                        return wide[q, 3 + s + ds, low : low + ROWS, :]

                    first = None
                    both = None
                    for reach in (1, 2, 3):
                        up, down = at(reach, 0), at(-reach, 0)
                        diff = up - down
                        total = (up + down) + (at(0, reach) + at(0, -reach))
                        if FIRST[reach - 1] != 1:
                            diff = diff * float(FIRST[reach - 1])
                        total = total * float(SECOND[reach - 1])
                        first = diff if first is None else first + diff
                        both = total if both is None else both + total
                    start = (2 * q + half) * normal + ROWS * tile
                    crow = slice(start, start + ROWS)
                    chord_first = chord[slot, crow, 0:LANES]
                    chord_second = chord[slot, crow, LANES : 2 * LANES]
                    both = both + (centre[q] * float(2 * CENTRE) + chord_second)
                    value = a * first + b * chord_first + g * both
                    for e in range(count):
                        value = value + couple[q][e] * centre[e]
                    if second:
                        value = value + 0.5 * before[q, s, rows, :]
                    result[q, s, rows, :] = value
                    if second and q == 0:
                        hit = jnp.where(lane == te_ref[s], value, 0.0)
                        column = jnp.sum(hit, axis=1, keepdims=True)
                        columns[rows, :] += jnp.where(lane == s, column, 0.0)
                    if not second:
                        station = lax.rem(s, 16)
                        moved = pltpu.roll(value, lax.rem(3 + 8 * station, LANES), 1)
                        kept = cells[q, lax.div(p, 8), rows, :]
                        cells[q, lax.div(p, 8), rows, :] = jnp.where(
                            lax.div(lane, 8) == station, moved, kept
                        )
        out_copy(p).start()
        return carry

    def out_copy(p):
        two = pl.ds(2 * p, 2)
        return pltpu.make_async_copy(result.at[:, two], out_hbm.at[:, two], out_sem.at[p])

    def arrive(c):
        for copy in copies(c):
            copy.wait()

    arrive(0)
    matmuls(0)
    for c in range(chunks):
        if c + 1 < chunks:
            arrive(c + 1)
        lax.fori_loop(c * pairs // chunks, (c + 1) * pairs // chunks, body, 0)

    if second:
        amp = fine_dot(columns[...].T, band_ref[...])
        amps[...] = amp[:stations].astype(BF16).astype(F32)
        lane4 = lax.div(lax.broadcasted_iota(jnp.int32, (4, LANES), 1), 16)
        pieces = [jnp.zeros((4, LANES), F32) for _ in range(8)]
        for u in range(8):
            some = amps[pl.ds(u, 4, stride=8), :]
            for j in range(8):
                shift = (16 * (u - j)) % LANES
                moved = pltpu.roll(some, shift, 1) if shift else some
                pieces[j] = jnp.where(lane4 == u, moved, pieces[j])
        for j in range(8):
            amp_out[j] = pieces[j]
    else:
        cells_out[...] = cells[...].astype(BF16)
        low_out[...] = result[:, 0:3].astype(BF16)
        high_out[...] = result[:, stations - 3 : stations].astype(BF16)

    def drain(p, carry):
        out_copy(p).wait()
        return carry

    lax.fori_loop(0, pairs, drain, 0)


def section(state, halos, fields, mixing, table, flow=None, te_local=None, band_table=None):
    count, stations, normal, _ = state.shape
    second = flow is not None
    pairs = stations // 2
    hbm = pl.BlockSpec(memory_space=pltpu.HBM)
    vmem = pl.BlockSpec(memory_space=pltpu.VMEM)
    smem = pl.BlockSpec(memory_space=pltpu.SMEM)
    args = [state, *halos, *fields, mixing, table]
    specs = [hbm] + [vmem] * 4 + [hbm] * 3 + [smem, vmem]
    shapes = [jax.ShapeDtypeStruct(state.shape, F32)]
    if second:
        args += [flow, te_local, band_table]
        specs += [hbm, smem, vmem]
        shapes.append(jax.ShapeDtypeStruct((8, 4, LANES), F32))
    else:
        shapes += [jax.ShapeDtypeStruct((count, 3, normal, LANES), BF16)] * 2
        shapes.append(jax.ShapeDtypeStruct((count, stations // 16, normal, LANES), BF16))
    field = pltpu.VMEM((stations, normal, LANES), BF16)
    args = [
        pltpu.with_memory_space_constraint(x, pltpu.HBM) if spec is hbm else x
        for x, spec in zip(args, specs)
    ]
    scratch = [
        pltpu.VMEM((count, stations + 6, normal + 16, LANES), F32),
        pltpu.VMEM((count, stations, normal, LANES), F32),
        pltpu.VMEM((2, count * 2 * normal, 2 * LANES), F32),
        pltpu.VMEM((count, stations // 16, normal, LANES), F32),
        pltpu.VMEM((count, stations // 16, normal, LANES), F32),
        field,
        field,
        field,
        pltpu.SemaphoreType.DMA((4, 4)),
        pltpu.SemaphoreType.DMA((pairs,)),
    ]
    if second:
        scratch += [
            pltpu.VMEM((count, stations, normal, LANES), F32),
            pltpu.SemaphoreType.DMA((4,)),
            pltpu.VMEM((normal, LANES), F32),
            pltpu.VMEM((stations, LANES), F32),
        ]
    return pl.pallas_call(
        functools.partial(section_kernel, second=second),
        out_shape=tuple(shapes),
        in_specs=specs,
        out_specs=tuple([hbm] + [vmem] * (len(shapes) - 1)),
        scratch_shapes=scratch,
        compiler_params=pltpu.CompilerParams(vmem_limit_bytes=40 << 20),
        cost_estimate=pl.CostEstimate(
            flops=60000000, transcendentals=0, bytes_accessed=12000000
        ),
        name="section_two" if second else "section_one",
    )(*args)


def spectra_kernel(spectra_ref, wanted_ref, own_ref, send_ref):
    stations, bands, slots = spectra_ref.shape
    width = wanted_ref.shape[1]
    rows = spectra_ref[...].astype(F32).reshape(stations * bands, slots).astype(BF16)
    slot = lax.broadcasted_iota(jnp.int32, (slots, width), 0)
    choose = jnp.where(slot == wanted_ref[...], 1.0, 0.0).astype(BF16)
    got = jnp.dot(rows, choose, preferred_element_type=F32)
    row_band = lax.rem(lax.broadcasted_iota(jnp.int32, got.shape, 0), bands)
    lane_band = lax.div(lax.broadcasted_iota(jnp.int32, got.shape, 1), width // bands)
    got = jnp.where(row_band == lane_band, got, 0.0).reshape(stations, bands, width)
    packed = jnp.sum(got, axis=1).astype(BF16)
    own_ref[...] = packed
    for d in range(send_ref.shape[0]):
        send_ref[d] = packed


def gram_kernel(prior_ref, every_ref, own_ref, ramp_ref, amp_ref, where_ref, rep_ref, out_ref, left):
    step = pl.program_id(0)
    bands, stations, tile = prior_ref.shape[1:]
    width = own_ref.shape[1]
    sources = amp_ref.shape[0] // (tile // stations) // pl.num_programs(0)

    def spread(source):
        whole = amp_ref[pl.ds(source * sources, sources)].astype(F32)
        total = whole[0]
        for j in range(1, sources):
            total = total + whole[j]
        lane = lax.div(lax.broadcasted_iota(jnp.int32, (8, LANES), 1), 16)
        here = lane == lax.broadcasted_iota(jnp.int32, (8, LANES), 0)
        rows = [
            jnp.where(here, jnp.broadcast_to(total[t : t + 1, :], (8, LANES)), 0.0)
            for t in range(4)
        ]
        return jnp.concatenate(rows).astype(BF16)

    @pl.when(step == 0)
    def _():
        own = own_ref[...].astype(F32)
        ramp = ramp_ref[...]
        lane = lax.broadcasted_iota(jnp.int32, own.shape, 1)
        real = lax.rem(lane, 32) < 16
        turned = jnp.where(
            real, pltpu.roll(own, width - 16, 1), -pltpu.roll(own, 16, 1)
        )
        mine = spread(where_ref[0])
        place = lax.broadcasted_iota(jnp.int32, (stations, LANES), 1)
        for c, part in enumerate((own, turned)):
            part = part * ramp
            high = part.astype(BF16).astype(F32)
            low = part - high
            amp = jnp.dot(mine, rep_ref[c], preferred_element_type=F32)
            for b in range(bands):
                at = (c * bands + b) * stations
                keep = lax.div(lane, 32) == b
                rows = slice(at, at + stations)
                left[rows, 0:width] = jnp.where(keep, high, 0.0).astype(BF16)
                left[rows, width : 2 * width] = jnp.where(keep, low, 0.0).astype(BF16)
                left[rows, 2 * width : 2 * width + LANES] = jnp.where(
                    lax.rem(place, 8) == b, amp, 0.0
                ).astype(BF16)

    blocks = tile // stations
    right = jnp.concatenate([spread(step * blocks + i) for i in range(blocks)])
    stored = every_ref[...]
    got = nt_dot(left[...], jnp.concatenate([stored, stored, right], axis=1))
    out_ref[...] = DECAY * prior_ref[...] + got.reshape(2, bands, stations, tile)


def amplitude_tables():
    index = np.arange(LANES)
    same = (index[:, None] % 16 == index[None, :] % 16).astype(np.float32)
    other = (index[:, None] % 8 == index[None, :] % 8) & (
        (index[:, None] % 16) // 8 != (index[None, :] % 16) // 8
    )
    sign = np.where((index % 16) // 8 == 0, 1.0, -1.0)
    return np.stack([same, other * sign[None, :]]).astype(ml_dtypes.bfloat16)


def shards(
    flow_state,
    vel_span,
    vel_chord,
    viscosity,
    mixing,
    te_index,
    band_response,
    spectra,
    offsets,
    prior_gram_blocks,
):
    count, stations, normal, cells = flow_state.shape
    bands, slots = spectra.shape[1], spectra.shape[2] // 2
    segs = offsets.shape[0]
    span_n, chord_n = lax.axis_size("span"), lax.axis_size("chord")
    span_pos, chord_pos = lax.axis_index("span"), lax.axis_index("chord")
    table = chord_matrices()
    fields = (vel_span, vel_chord, viscosity)

    def exchange(low, high, edge):
        up = [(i, (i + 1) % span_n) for i in range(span_n)]
        down = [(b, a) for a, b in up]
        forward = [(i, i + 1) for i in range(chord_n - 1)]
        backward = [(b, a) for a, b in forward]
        return (
            lax.ppermute(high, "span", up),
            lax.ppermute(low, "span", down),
            lax.ppermute(edge, "chord", forward),
            lax.ppermute(edge, "chord", backward),
        )

    edge_shape = jax.ShapeDtypeStruct((count, stations // 16, normal, LANES), BF16)
    ends_shape = jax.ShapeDtypeStruct((count, 3, normal, LANES), BF16)

    def per_quantity(shape):
        return pl.BlockSpec((1,) + shape.shape[1:], lambda q: (q, 0, 0, 0))

    edge, low, high = pl.pallas_call(
        edges_kernel,
        grid=(count,),
        out_shape=(edge_shape, ends_shape, ends_shape),
        in_specs=[per_quantity(flow_state)],
        out_specs=(per_quantity(edge_shape), per_quantity(ends_shape), per_quantity(ends_shape)),
        name="edges",
    )(flow_state)
    halos = exchange(low, high, edge)

    width = bands * 2 * segs
    wanted = jnp.tile(jnp.concatenate([offsets, offsets + slots]), bands)[None]
    packed, send = pl.pallas_call(
        spectra_kernel,
        out_shape=(
            jax.ShapeDtypeStruct((stations, width), BF16),
            jax.ShapeDtypeStruct((span_n, stations, width), BF16),
        ),
        name="spectra",
    )(spectra, wanted)
    every = lax.all_to_all(send, "span", 0, 0, tiled=True).reshape(span_n * stations, width)

    (section_one, low, high, edge) = section(flow_state, halos, fields, mixing, table)
    halos = exchange(low, high, edge)

    te_local = te_index - chord_pos * cells
    band_table = band_response.reshape(normal, 2, chord_n, bands).transpose(0, 2, 1, 3)
    band_table = band_table.reshape(normal, chord_n * 2 * bands)
    flow_next, amps = section(
        section_one,
        halos,
        fields,
        mixing,
        table,
        flow=flow_state,
        te_local=te_local,
        band_table=band_table,
    )
    amps = jnp.broadcast_to(amps.astype(BF16)[None], (span_n,) + amps.shape)
    amps = lax.all_to_all(
        amps.reshape((span_n * chord_n,) + amps.shape[2:]), ("span", "chord"), 0, 0, tiled=True
    )

    ramp = np.tile((np.arange(segs, dtype=np.float32) + 1) / segs, 2 * bands)[None]
    tiles = 4
    tile = span_n * stations // tiles
    gram_block = pl.BlockSpec((2, bands, stations, tile), lambda t: (0, 0, 0, t))

    def whole(x):
        return pl.BlockSpec(x.shape, lambda t: (0,) * x.ndim)

    reps = amplitude_tables()
    gram_next = pl.pallas_call(
        gram_kernel,
        grid=(tiles,),
        out_shape=jax.ShapeDtypeStruct(prior_gram_blocks.shape, F32),
        in_specs=[
            gram_block,
            pl.BlockSpec((tile, width), lambda t: (t, 0)),
            whole(packed),
            whole(ramp),
            whole(amps),
            pl.BlockSpec(memory_space=pltpu.SMEM),
            whole(reps),
        ],
        out_specs=gram_block,
        scratch_shapes=[pltpu.VMEM((2 * bands * stations, 2 * width + LANES), BF16)],
        compiler_params=pltpu.CompilerParams(vmem_limit_bytes=32 << 20),
        name="gram",
    )(prior_gram_blocks, every, packed, ramp, amps, span_pos.reshape(1), reps)
    return (flow_next, gram_next)


def solution(mesh):
    return jax.shard_map(
        shards,
        mesh=mesh,
        in_specs=(
            P(None, "span", None, "chord"),
            P("span", None, "chord"),
            P("span", None, "chord"),
            P("span", None, "chord"),
            P(),
            P("span"),
            P(),
            P("span", "chord", None),
            P(),
            P(None, "chord", "span", None),
        ),
        out_specs=(P(None, "span", None, "chord"), P(None, "chord", "span", None)),
        check_vma=False,
    )
```

```python
import functools

import jax
import jax.numpy as jnp
import ml_dtypes
import numpy as np
from jax import lax
from jax.experimental import pallas as pl
from jax.experimental.pallas import tpu as pltpu
from jax.sharding import PartitionSpec as P

FIRST = (45, -9, 1)
SECOND = (270, -27, 2)
CENTRE = -490
TIME_STEP = 0.6
DECAY = 0.9
F32 = jnp.float32
BF16 = jnp.bfloat16
LANES = 128


def chord_matrices():
    inner = np.zeros((LANES, 2 * LANES), np.float32)
    outer = np.zeros((LANES, 2 * LANES), np.float32)

    def row(cell):
        if cell < 0:
            return outer, cell + 3
        if cell >= LANES:
            return outer, cell - LANES + 3
        return inner, cell

    for cell in range(LANES):
        inner[cell, LANES + cell] += CENTRE
        for reach in (1, 2, 3):
            for sign in (1, -1):
                table, index = row(cell + sign * reach)
                table[index, cell] += sign * FIRST[reach - 1]
                table[index, LANES + cell] += SECOND[reach - 1]
    return np.concatenate([inner, inner, outer]).astype(ml_dtypes.bfloat16)


def nt_dot(a, b):
    return lax.dot_general(a, b, (((1,), (1,)), ((), ())), preferred_element_type=F32)


def fine_dot(a, b):
    def pieces(x):
        one = x.astype(BF16)
        x = x - one.astype(F32)
        two = x.astype(BF16)
        return one, two, (x - two.astype(F32)).astype(BF16)

    left, right = pieces(a), pieces(b)
    total = None
    for i, j in ((2, 0), (0, 2), (1, 1), (1, 0), (0, 1), (0, 0)):
        part = jnp.dot(left[i], right[j], preferred_element_type=F32)
        total = part if total is None else total + part
    return total


def edge_lanes(shape):
    return lax.div(lax.broadcasted_iota(jnp.int32, shape, len(shape) - 1), 8)


def edges_kernel(flow_ref, cells_ref, low_ref, high_ref):
    stations, normal = flow_ref.shape[1:3]
    lane = edge_lanes((16, LANES))
    for half in range(stations // 16):
        for tile in range(normal // 16):
            rows = slice(16 * tile, 16 * tile + 16)
            packed = jnp.zeros((16, LANES), F32)
            for s in range(16):
                moved = pltpu.roll(flow_ref[0, 16 * half + s, rows, :], (3 + 8 * s) % LANES, 1)
                packed = jnp.where(lane == s, moved, packed)
            cells_ref[0, half, rows, :] = packed.astype(BF16)
    low_ref[0] = flow_ref[0, 0:3].astype(BF16)
    high_ref[0] = flow_ref[0, stations - 3 : stations].astype(BF16)


def section_kernel(*refs, second):
    take = list(refs).pop
    refs = list(refs)
    take = refs.pop
    state_hbm = take(0)
    halo_hbm = [take(0) for _ in range(4)]
    vs_hbm, vc_hbm, nu_hbm = (take(0) for _ in range(3))
    mix, table_ref = take(0), take(0)
    if second:
        flow_hbm, te_ref, band_ref = (take(0) for _ in range(3))
    out_hbm = take(0)
    if second:
        amp_out = take(0)
    else:
        low_out, high_out, cells_out = (take(0) for _ in range(3))
    wide, result, chord_a, chord_b, halos, cells, vs, vc, nu, in_sem, out_sem = (take(0) for _ in range(11))
    if second:
        before, before_sem, columns, amps = (take(0) for _ in range(4))
    span_low, span_high, chord_low, chord_high, halo_sem = (take(0) for _ in range(5))

    count, stations, normal = wide.shape[0], vs.shape[0], vs.shape[1]
    chunks, pairs = 8, stations // 2
    per = stations // chunks

    def copies(c):
        rows = pl.ds(per * c, per)
        todo = [
            pltpu.make_async_copy(
                state_hbm.at[:, rows],
                wide.at[:, pl.ds(3 + per * c, per), pl.ds(8, normal), :],
                in_sem.at[0, c],
            ),
            pltpu.make_async_copy(vs_hbm.at[rows], vs.at[rows], in_sem.at[1, c]),
            pltpu.make_async_copy(vc_hbm.at[rows], vc.at[rows], in_sem.at[2, c]),
            pltpu.make_async_copy(nu_hbm.at[rows], nu.at[rows], in_sem.at[3, c]),
        ]
        if second:
            todo.append(
                pltpu.make_async_copy(flow_hbm.at[:, rows], before.at[:, rows], before_sem.at[c])
            )
        return todo

    halo_copies = [
        pltpu.make_async_copy(source, target, halo_sem.at[i])
        for i, (source, target) in enumerate(
            zip(halo_hbm, (span_low, span_high, chord_low, chord_high))
        )
    ]
    for copy in halo_copies:
        copy.start()
    for c in range(chunks):
        for copy in copies(c):
            copy.start()

    nothing = jnp.zeros((count, stations, 8, LANES), F32)
    wide[:, 3 : 3 + stations, 0:8, :] = nothing
    wide[:, 3 : 3 + stations, 8 + normal : 16 + normal, :] = nothing
    if second:
        columns[...] = jnp.zeros(columns.shape, F32)
    for copy in halo_copies:
        copy.wait()
    wide[:, 0:3, 8 : 8 + normal, :] = span_low[...].astype(F32)
    wide[:, 3 + stations : 6 + stations, 8 : 8 + normal, :] = span_high[...].astype(F32)
    place = lax.rem(lax.broadcasted_iota(jnp.int32, (normal, LANES), 1), 8)
    for q in range(count):
        for half in range(stations // 16):
            near = jnp.where(
                place < 3, chord_low[q, half].astype(F32), chord_high[q, half].astype(F32)
            )
            halos[q, half] = jnp.where(place < 6, near, 0.0)

    def matmuls(p, chord):
        half = lax.div(p, 8)
        parts = []
        for q in range(count):
            for d in range(2):
                slab = wide[q, 3 + 2 * p + d, 8 : 8 + normal, :]
                high = slab.astype(BF16)
                low = (slab - high.astype(F32)).astype(BF16)
                shift = lax.rem(LANES - 8 * lax.rem(2 * p + d, 16), LANES)
                beyond = pltpu.roll(halos[q, half], shift, 1).astype(BF16)
                parts.append(jnp.concatenate([high, low, beyond], axis=1))
        chord[...] = jnp.dot(
            jnp.concatenate(parts), table_ref[...], preferred_element_type=F32
        )

    scale = 0.5 if second else 1.0
    couple = [
        [scale * ((1.0 if q == e else 0.0) + TIME_STEP * mix[q, e]) for e in range(count)]
        for q in range(count)
    ]
    ROWS = 16
    lane = lax.broadcasted_iota(jnp.int32, (ROWS, LANES), 1)

    def body(i, carry):
        pair(2 * i, chord_a, chord_b)
        pair(2 * i + 1, chord_b, chord_a)
        return carry

    def pair(p, chord, later):
        matmuls(jnp.minimum(p + 1, pairs - 1), later)
        for half in range(2):
            s = 2 * p + half
            for tile in range(normal // ROWS):
                rows = slice(ROWS * tile, ROWS * tile + ROWS)
                a = vs[s, rows, :].astype(F32) * (-scale * TIME_STEP / 60)
                b = vc[s, rows, :].astype(F32) * (-scale * TIME_STEP / 60)
                g = nu[s, rows, :].astype(F32) * (scale * TIME_STEP / 180)
                centre = [
                    wide[e, 3 + s, 8 + ROWS * tile : 8 + ROWS * tile + ROWS, :]
                    for e in range(count)
                ]
                for q in range(count):

                    def at(ds, dn):
                        low = 8 + ROWS * tile + dn
                        return wide[q, 3 + s + ds, low : low + ROWS, :]

                    first = None
                    both = None
                    for reach in (1, 2, 3):
                        up, down = at(reach, 0), at(-reach, 0)
                        diff = up - down
                        total = (up + down) + (at(0, reach) + at(0, -reach))
                        if FIRST[reach - 1] != 1:
                            diff = diff * float(FIRST[reach - 1])
                        total = total * float(SECOND[reach - 1])
                        first = diff if first is None else first + diff
                        both = total if both is None else both + total
                    start = (2 * q + half) * normal + ROWS * tile
                    crow = slice(start, start + ROWS)
                    chord_first = chord[crow, 0:LANES]
                    chord_second = chord[crow, LANES : 2 * LANES]
                    both = both + (centre[q] * float(2 * CENTRE) + chord_second)
                    value = a * first + b * chord_first + g * both
                    for e in range(count):
                        value = value + couple[q][e] * centre[e]
                    if second:
                        value = value + 0.5 * before[q, s, rows, :]
                    result[q, s, rows, :] = value
                    if second and q == 0:
                        hit = jnp.where(lane == te_ref[s], value, 0.0)
                        column = jnp.sum(hit, axis=1, keepdims=True)
                        columns[rows, :] += jnp.where(lane == s, column, 0.0)
                    if not second:
                        station = lax.rem(s, 16)
                        moved = pltpu.roll(value, lax.rem(3 + 8 * station, LANES), 1)
                        kept = cells[q, lax.div(p, 8), rows, :]
                        cells[q, lax.div(p, 8), rows, :] = jnp.where(
                            lax.div(lane, 8) == station, moved, kept
                        )
        out_copy(p).start()

    def out_copy(p):
        two = pl.ds(2 * p, 2)
        return pltpu.make_async_copy(result.at[:, two], out_hbm.at[:, two], out_sem.at[p])

    def arrive(c):
        for copy in copies(c):
            copy.wait()

    arrive(0)
    matmuls(0, chord_a)
    for c in range(chunks):
        if c + 1 < chunks:
            arrive(c + 1)
        lax.fori_loop(c * pairs // chunks // 2, (c + 1) * pairs // chunks // 2, body, 0)

    if second:
        amp = fine_dot(columns[...].T, band_ref[...])
        amps[...] = amp[:stations].astype(BF16).astype(F32)
        lane4 = lax.div(lax.broadcasted_iota(jnp.int32, (4, LANES), 1), 16)
        pieces = [jnp.zeros((4, LANES), F32) for _ in range(8)]
        for u in range(8):
            some = amps[pl.ds(u, 4, stride=8), :]
            for j in range(8):
                shift = (16 * (u - j)) % LANES
                moved = pltpu.roll(some, shift, 1) if shift else some
                pieces[j] = jnp.where(lane4 == u, moved, pieces[j])
        for j in range(8):
            amp_out[j] = pieces[j]
    else:
        cells_out[...] = cells[...].astype(BF16)
        low_out[...] = result[:, 0:3].astype(BF16)
        high_out[...] = result[:, stations - 3 : stations].astype(BF16)

    def drain(p, carry):
        out_copy(p).wait()
        return carry

    lax.fori_loop(0, pairs, drain, 0)


def section(state, halos, fields, mixing, table, flow=None, te_local=None, band_table=None):
    count, stations, normal, _ = state.shape
    second = flow is not None
    pairs = stations // 2
    hbm = pl.BlockSpec(memory_space=pltpu.HBM)
    vmem = pl.BlockSpec(memory_space=pltpu.VMEM)
    smem = pl.BlockSpec(memory_space=pltpu.SMEM)
    args = [state, *halos, *fields, mixing, table]
    specs = [hbm] * 8 + [smem, vmem]
    shapes = [jax.ShapeDtypeStruct(state.shape, F32)]
    if second:
        args += [flow, te_local, band_table]
        specs += [hbm, smem, vmem]
        shapes.append(jax.ShapeDtypeStruct((8, 4, LANES), F32))
    else:
        shapes += [jax.ShapeDtypeStruct((count, 3, normal, LANES), BF16)] * 2
        shapes.append(jax.ShapeDtypeStruct((count, stations // 16, normal, LANES), BF16))
    field = pltpu.VMEM((stations, normal, LANES), BF16)
    args = [
        pltpu.with_memory_space_constraint(x, pltpu.HBM) if spec is hbm and not (second and x is state) else x
        for x, spec in zip(args, specs)
    ]
    scratch = [
        pltpu.VMEM((count, stations + 6, normal + 16, LANES), F32),
        pltpu.VMEM((count, stations, normal, LANES), F32),
        pltpu.VMEM((count * 2 * normal, 2 * LANES), F32),
        pltpu.VMEM((count * 2 * normal, 2 * LANES), F32),
        pltpu.VMEM((count, stations // 16, normal, LANES), F32),
        pltpu.VMEM((count, stations // 16, normal, LANES), F32),
        field,
        field,
        field,
        pltpu.SemaphoreType.DMA((4, 8)),
        pltpu.SemaphoreType.DMA((pairs,)),
    ]
    if second:
        scratch += [
            pltpu.VMEM((count, stations, normal, LANES), F32),
            pltpu.SemaphoreType.DMA((8,)),
            pltpu.VMEM((normal, LANES), F32),
            pltpu.VMEM((stations, LANES), F32),
        ]
    scratch += [pltpu.VMEM((count, 3, normal, LANES), BF16)] * 2
    scratch += [pltpu.VMEM((count, stations // 16, normal, LANES), BF16)] * 2
    scratch.append(pltpu.SemaphoreType.DMA((4,)))
    return pl.pallas_call(
        functools.partial(section_kernel, second=second),
        out_shape=tuple(shapes),
        in_specs=specs,
        out_specs=tuple([hbm] + [vmem] * (len(shapes) - 1)),
        scratch_shapes=scratch,
        compiler_params=pltpu.CompilerParams(vmem_limit_bytes=20 << 20),
        cost_estimate=pl.CostEstimate(
            flops=60000000, transcendentals=0, bytes_accessed=12000000
        ),
        name="section_two" if second else "section_one",
    )(*args)


def spectra_kernel(spectra_ref, wanted_ref, own_ref, send_ref):
    stations, bands, slots = spectra_ref.shape
    width = wanted_ref.shape[1]
    rows = spectra_ref[...].astype(F32).reshape(stations * bands, slots).astype(BF16)
    slot = lax.broadcasted_iota(jnp.int32, (slots, width), 0)
    choose = jnp.where(slot == wanted_ref[...], 1.0, 0.0).astype(BF16)
    got = jnp.dot(rows, choose, preferred_element_type=F32)
    row_band = lax.rem(lax.broadcasted_iota(jnp.int32, got.shape, 0), bands)
    lane_band = lax.div(lax.broadcasted_iota(jnp.int32, got.shape, 1), width // bands)
    got = jnp.where(row_band == lane_band, got, 0.0).reshape(stations, bands, width)
    packed = jnp.sum(got, axis=1).astype(BF16)
    own_ref[...] = packed
    for d in range(send_ref.shape[0]):
        send_ref[d] = packed


def gram_kernel(prior_ref, every_ref, own_ref, ramp_ref, amp_ref, where_ref, rep_ref, out_ref, left):
    step = pl.program_id(0)
    bands, stations, tile = prior_ref.shape[1:]
    width = own_ref.shape[1]
    sources = amp_ref.shape[0] // (tile // stations) // pl.num_programs(0)

    def spread(source):
        whole = amp_ref[pl.ds(source * sources, sources)].astype(F32)
        total = whole[0]
        for j in range(1, sources):
            total = total + whole[j]
        lane = lax.div(lax.broadcasted_iota(jnp.int32, (8, LANES), 1), 16)
        here = lane == lax.broadcasted_iota(jnp.int32, (8, LANES), 0)
        rows = [
            jnp.where(here, jnp.broadcast_to(total[t : t + 1, :], (8, LANES)), 0.0)
            for t in range(4)
        ]
        return jnp.concatenate(rows).astype(BF16)

    @pl.when(step == 0)
    def _():
        own = own_ref[...].astype(F32)
        ramp = ramp_ref[...]
        lane = lax.broadcasted_iota(jnp.int32, own.shape, 1)
        real = lax.rem(lane, 32) < 16
        turned = jnp.where(
            real, pltpu.roll(own, width - 16, 1), -pltpu.roll(own, 16, 1)
        )
        mine = spread(where_ref[0])
        place = lax.broadcasted_iota(jnp.int32, (stations, LANES), 1)
        for c, part in enumerate((own, turned)):
            part = part * ramp
            high = part.astype(BF16).astype(F32)
            low = part - high
            amp = jnp.dot(mine, rep_ref[c], preferred_element_type=F32)
            for b in range(bands):
                at = (c * bands + b) * stations
                keep = lax.div(lane, 32) == b
                rows = slice(at, at + stations)
                left[rows, 0:width] = jnp.where(keep, high, 0.0).astype(BF16)
                left[rows, width : 2 * width] = jnp.where(keep, low, 0.0).astype(BF16)
                left[rows, 2 * width : 2 * width + LANES] = jnp.where(
                    lax.rem(place, 8) == b, amp, 0.0
                ).astype(BF16)

    blocks = tile // stations
    right = jnp.concatenate([spread(step * blocks + i) for i in range(blocks)])
    stored = every_ref[...]
    got = nt_dot(left[...], jnp.concatenate([stored, stored, right], axis=1))
    out_ref[...] = DECAY * prior_ref[...] + got.reshape(2, bands, stations, tile)


def amplitude_tables():
    index = np.arange(LANES)
    same = (index[:, None] % 16 == index[None, :] % 16).astype(np.float32)
    other = (index[:, None] % 8 == index[None, :] % 8) & (
        (index[:, None] % 16) // 8 != (index[None, :] % 16) // 8
    )
    sign = np.where((index % 16) // 8 == 0, 1.0, -1.0)
    return np.stack([same, other * sign[None, :]]).astype(ml_dtypes.bfloat16)


def shards(
    flow_state,
    vel_span,
    vel_chord,
    viscosity,
    mixing,
    te_index,
    band_response,
    spectra,
    offsets,
    prior_gram_blocks,
):
    count, stations, normal, cells = flow_state.shape
    bands, slots = spectra.shape[1], spectra.shape[2] // 2
    segs = offsets.shape[0]
    span_n, chord_n = lax.axis_size("span"), lax.axis_size("chord")
    span_pos, chord_pos = lax.axis_index("span"), lax.axis_index("chord")
    table = chord_matrices()
    fields = (vel_span, vel_chord, viscosity)

    def exchange(low, high, edge):
        up = [(i, (i + 1) % span_n) for i in range(span_n)]
        down = [(b, a) for a, b in up]
        forward = [(i, i + 1) for i in range(chord_n - 1)]
        backward = [(b, a) for a, b in forward]
        return (
            lax.ppermute(high, "span", up),
            lax.ppermute(low, "span", down),
            lax.ppermute(edge, "chord", forward),
            lax.ppermute(edge, "chord", backward),
        )

    width = bands * 2 * segs
    wanted = jnp.tile(jnp.concatenate([offsets, offsets + slots]), bands)[None]
    packed, send = pl.pallas_call(
        spectra_kernel,
        out_shape=(
            jax.ShapeDtypeStruct((stations, width), BF16),
            jax.ShapeDtypeStruct((span_n, stations, width), BF16),
        ),
        name="spectra",
    )(spectra, wanted)
    every = lax.all_to_all(send, "span", 0, 0, tiled=True).reshape(span_n * stations, width)

    edge_shape = jax.ShapeDtypeStruct((count, stations // 16, normal, LANES), BF16)
    ends_shape = jax.ShapeDtypeStruct((count, 3, normal, LANES), BF16)

    def per_quantity(shape):
        return pl.BlockSpec((1,) + shape.shape[1:], lambda q: (q, 0, 0, 0))

    edge, low, high = pl.pallas_call(
        edges_kernel,
        grid=(count,),
        out_shape=(edge_shape, ends_shape, ends_shape),
        in_specs=[per_quantity(flow_state)],
        out_specs=(per_quantity(edge_shape), per_quantity(ends_shape), per_quantity(ends_shape)),
        name="edges",
    )(flow_state)
    halos = exchange(low, high, edge)

    (section_one, low, high, edge) = section(flow_state, halos, fields, mixing, table)
    halos = exchange(low, high, edge)
    halos, every = lax.optimization_barrier((halos, every))

    te_local = te_index - chord_pos * cells
    band_table = band_response.reshape(normal, 2, chord_n, bands).transpose(0, 2, 1, 3)
    band_table = band_table.reshape(normal, chord_n * 2 * bands)
    flow_next, amps = section(
        section_one,
        halos,
        fields,
        mixing,
        table,
        flow=flow_state,
        te_local=te_local,
        band_table=band_table,
    )
    amps = jnp.broadcast_to(amps.astype(BF16)[None], (span_n,) + amps.shape)
    amps = lax.all_to_all(
        amps.reshape((span_n * chord_n,) + amps.shape[2:]), ("span", "chord"), 0, 0, tiled=True
    )

    ramp = np.tile((np.arange(segs, dtype=np.float32) + 1) / segs, 2 * bands)[None]
    tiles = 4
    tile = span_n * stations // tiles
    gram_block = pl.BlockSpec((2, bands, stations, tile), lambda t: (0, 0, 0, t))

    def whole(x):
        return pl.BlockSpec(x.shape, lambda t: (0,) * x.ndim)

    reps = amplitude_tables()
    gram_next = pl.pallas_call(
        gram_kernel,
        grid=(tiles,),
        out_shape=jax.ShapeDtypeStruct(prior_gram_blocks.shape, F32),
        in_specs=[
            gram_block,
            pl.BlockSpec((tile, width), lambda t: (t, 0)),
            whole(packed),
            whole(ramp),
            whole(amps),
            pl.BlockSpec(memory_space=pltpu.SMEM),
            whole(reps),
        ],
        out_specs=gram_block,
        scratch_shapes=[pltpu.VMEM((2 * bands * stations, 2 * width + LANES), BF16)],
        compiler_params=pltpu.CompilerParams(vmem_limit_bytes=32 << 20),
        name="gram",
    )(
        pltpu.with_memory_space_constraint(prior_gram_blocks, pltpu.HBM),
        pltpu.with_memory_space_constraint(every, pltpu.HBM),
        packed,
        ramp,
        amps,
        span_pos.reshape(1),
        reps,
    )
    return (flow_next, gram_next)


def solution(mesh):
    return jax.shard_map(
        shards,
        mesh=mesh,
        in_specs=(
            P(None, "span", None, "chord"),
            P("span", None, "chord"),
            P("span", None, "chord"),
            P("span", None, "chord"),
            P(),
            P("span"),
            P(),
            P("span", "chord", None),
            P(),
            P(None, "chord", "span", None),
        ),
        out_specs=(P(None, "span", None, "chord"), P(None, "chord", "span", None)),
        check_vma=False,
    )
```

```python
import functools

import jax
import jax.numpy as jnp
import ml_dtypes
import numpy as np
from jax import lax
from jax.experimental import pallas as pl
from jax.experimental.pallas import tpu as pltpu
from jax.sharding import PartitionSpec as P

FIRST = (45, -9, 1)
SECOND = (270, -27, 2)
CENTRE = -490
TIME_STEP = 0.6
DECAY = 0.9
F32 = jnp.float32
BF16 = jnp.bfloat16
LANES = 128


def chord_matrices():
    inner = np.zeros((LANES, 2 * LANES), np.float32)
    outer = np.zeros((LANES, 2 * LANES), np.float32)

    def row(cell):
        if cell < 0:
            return outer, cell + 3
        if cell >= LANES:
            return outer, cell - LANES + 3
        return inner, cell

    for cell in range(LANES):
        inner[cell, LANES + cell] += CENTRE
        for reach in (1, 2, 3):
            for sign in (1, -1):
                table, index = row(cell + sign * reach)
                table[index, cell] += sign * FIRST[reach - 1]
                table[index, LANES + cell] += SECOND[reach - 1]
    return np.concatenate([inner, inner, outer]).astype(ml_dtypes.bfloat16)


def nt_dot(a, b):
    return lax.dot_general(a, b, (((1,), (1,)), ((), ())), preferred_element_type=F32)


def fine_dot(a, b):
    def pieces(x):
        one = x.astype(BF16)
        x = x - one.astype(F32)
        two = x.astype(BF16)
        return one, two, (x - two.astype(F32)).astype(BF16)

    left, right = pieces(a), pieces(b)
    total = None
    for i, j in ((2, 0), (0, 2), (1, 1), (1, 0), (0, 1), (0, 0)):
        part = jnp.dot(left[i], right[j], preferred_element_type=F32)
        total = part if total is None else total + part
    return total


def edge_lanes(shape):
    return lax.div(lax.broadcasted_iota(jnp.int32, shape, len(shape) - 1), 8)


def edges_kernel(flow_ref, cells_ref, low_ref, high_ref):
    stations, normal = flow_ref.shape[1:3]
    lane = edge_lanes((16, LANES))
    for half in range(stations // 16):
        for tile in range(normal // 16):
            rows = slice(16 * tile, 16 * tile + 16)
            packed = jnp.zeros((16, LANES), F32)
            for s in range(16):
                moved = pltpu.roll(flow_ref[0, 16 * half + s, rows, :], (3 + 8 * s) % LANES, 1)
                packed = jnp.where(lane == s, moved, packed)
            cells_ref[0, half, rows, :] = packed.astype(BF16)
    low_ref[0] = flow_ref[0, 0:3].astype(BF16)
    high_ref[0] = flow_ref[0, stations - 3 : stations].astype(BF16)


def section_kernel(*refs, second, profile, carried, quantities):
    refs = list(refs)
    take = refs.pop
    state_ref = take(0)
    halo_hbm = [take(0) for _ in range(4)]
    vs_hbm, vc_hbm, nu_hbm = (take(0) for _ in range(3))
    mix, table_ref = take(0), take(0)
    if second:
        flow_hbm = take(0)
    if profile:
        te_ref, band_ref = take(0), take(0)
    if carried:
        take(0)
    out_hbm = take(0)
    if profile:
        amp_out = take(0)
    if not second:
        low_out, high_out, cells_out = (take(0) for _ in range(3))
    wide, result, chord_a, chord_b, halos, cells, vs, vc, nu, in_sem, out_sem = (take(0) for _ in range(11))
    if second:
        before, before_sem = take(0), take(0)
    if profile:
        columns, amps = take(0), take(0)
    span_low, span_high, chord_low, chord_high, halo_sem = (take(0) for _ in range(5))

    count, stations, normal = len(quantities), vs.shape[0], vs.shape[1]
    everything = range(state_ref.shape[0])
    some = pl.ds(quantities[0], count)
    chunks, pairs = 8, stations // 2
    per = stations // chunks

    def copies(c):
        rows = pl.ds(per * c, per)
        todo = [
            pltpu.make_async_copy(
                state_ref.at[some, rows],
                wide.at[:, pl.ds(3 + per * c, per), pl.ds(8, normal), :],
                in_sem.at[0, c],
            ),
            pltpu.make_async_copy(vs_hbm.at[rows], vs.at[rows], in_sem.at[1, c]),
            pltpu.make_async_copy(vc_hbm.at[rows], vc.at[rows], in_sem.at[2, c]),
            pltpu.make_async_copy(nu_hbm.at[rows], nu.at[rows], in_sem.at[3, c]),
        ]
        if second:
            todo.append(
                pltpu.make_async_copy(flow_hbm.at[some, rows], before.at[:, rows], before_sem.at[c])
            )
        return todo

    halo_copies = [
        pltpu.make_async_copy(source, target, halo_sem.at[i])
        for i, (source, target) in enumerate(
            zip(halo_hbm, (span_low, span_high, chord_low, chord_high))
        )
    ]
    for copy in halo_copies:
        copy.start()
    for c in range(chunks):
        for copy in copies(c):
            copy.start()

    nothing = jnp.zeros((count, stations, 8, LANES), F32)
    wide[:, 3 : 3 + stations, 0:8, :] = nothing
    wide[:, 3 : 3 + stations, 8 + normal : 16 + normal, :] = nothing
    if profile:
        columns[...] = jnp.zeros(columns.shape, F32)
    for copy in halo_copies:
        copy.wait()
    wide[:, 0:3, 8 : 8 + normal, :] = span_low[some].astype(F32)
    wide[:, 3 + stations : 6 + stations, 8 : 8 + normal, :] = span_high[some].astype(F32)
    place = lax.rem(lax.broadcasted_iota(jnp.int32, (normal, LANES), 1), 8)
    for local, q in enumerate(quantities):
        for half in range(stations // 16):
            near = jnp.where(
                place < 3, chord_low[q, half].astype(F32), chord_high[q, half].astype(F32)
            )
            halos[local, half] = jnp.where(place < 6, near, 0.0)

    def matmuls(p, chord):
        half = lax.div(p, 8)
        parts = []
        for q in range(count):
            for d in range(2):
                slab = wide[q, 3 + 2 * p + d, 8 : 8 + normal, :]
                high = slab.astype(BF16)
                low = (slab - high.astype(F32)).astype(BF16)
                shift = lax.rem(LANES - 8 * lax.rem(2 * p + d, 16), LANES)
                beyond = pltpu.roll(halos[q, half], shift, 1).astype(BF16)
                parts.append(jnp.concatenate([high, low, beyond], axis=1))
        chord[...] = jnp.dot(
            jnp.concatenate(parts), table_ref[...], preferred_element_type=F32
        )

    scale = 0.5 if second else 1.0
    couple = [
        [scale * ((1.0 if q == e else 0.0) + TIME_STEP * mix[q, e]) for e in everything]
        for q in quantities
    ]
    ROWS = 16
    lane = lax.broadcasted_iota(jnp.int32, (ROWS, LANES), 1)

    def body(i, carry):
        pair(2 * i, chord_a, chord_b)
        pair(2 * i + 1, chord_b, chord_a)
        return carry

    def pair(p, chord, later):
        matmuls(jnp.minimum(p + 1, pairs - 1), later)
        for half in range(2):
            s = 2 * p + half
            for tile in range(normal // ROWS):
                rows = slice(ROWS * tile, ROWS * tile + ROWS)
                a = vs[s, rows, :].astype(F32) * (-scale * TIME_STEP / 60)
                b = vc[s, rows, :].astype(F32) * (-scale * TIME_STEP / 60)
                g = nu[s, rows, :].astype(F32) * (scale * TIME_STEP / 180)
                centre = [
                    wide[e - quantities[0], 3 + s, 8 + ROWS * tile : 8 + ROWS * tile + ROWS, :]
                    if e in quantities
                    else state_ref[e, s, rows, :]
                    for e in everything
                ]
                for local, q in enumerate(quantities):

                    def at(ds, dn):
                        low = 8 + ROWS * tile + dn
                        return wide[local, 3 + s + ds, low : low + ROWS, :]

                    first = None
                    both = None
                    for reach in (1, 2, 3):
                        up, down = at(reach, 0), at(-reach, 0)
                        diff = up - down
                        total = (up + down) + (at(0, reach) + at(0, -reach))
                        if FIRST[reach - 1] != 1:
                            diff = diff * float(FIRST[reach - 1])
                        total = total * float(SECOND[reach - 1])
                        first = diff if first is None else first + diff
                        both = total if both is None else both + total
                    start = (2 * local + half) * normal + ROWS * tile
                    crow = slice(start, start + ROWS)
                    chord_first = chord[crow, 0:LANES]
                    chord_second = chord[crow, LANES : 2 * LANES]
                    both = both + (centre[q] * float(2 * CENTRE) + chord_second)
                    value = a * first + b * chord_first + g * both
                    for e in everything:
                        value = value + couple[local][e] * centre[e]
                    if second:
                        value = value + 0.5 * before[local, s, rows, :]
                    result[local, s, rows, :] = value
                    if profile and q == 0:
                        hit = jnp.where(lane == te_ref[s], value, 0.0)
                        column = jnp.sum(hit, axis=1, keepdims=True)
                        columns[rows, :] += jnp.where(lane == s, column, 0.0)
                    if not second:
                        station = lax.rem(s, 16)
                        moved = pltpu.roll(value, lax.rem(3 + 8 * station, LANES), 1)
                        kept = cells[q, lax.div(p, 8), rows, :]
                        cells[q, lax.div(p, 8), rows, :] = jnp.where(
                            lax.div(lane, 8) == station, moved, kept
                        )
        out_copy(p).start()

    def out_copy(p):
        two = pl.ds(2 * p, 2)
        return pltpu.make_async_copy(result.at[:, two], out_hbm.at[some, two], out_sem.at[p])

    def arrive(c):
        for copy in copies(c):
            copy.wait()

    arrive(0)
    matmuls(0, chord_a)
    for c in range(chunks):
        if c + 1 < chunks:
            arrive(c + 1)
        lax.fori_loop(c * pairs // chunks // 2, (c + 1) * pairs // chunks // 2, body, 0)

    if profile:
        amp = fine_dot(columns[...].T, band_ref[...])
        amps[...] = amp[:stations].astype(BF16).astype(F32)
        lane4 = lax.div(lax.broadcasted_iota(jnp.int32, (4, LANES), 1), 16)
        pieces = [jnp.zeros((4, LANES), F32) for _ in range(8)]
        for u in range(8):
            taken = amps[pl.ds(u, 4, stride=8), :]
            for j in range(8):
                shift = (16 * (u - j)) % LANES
                moved = pltpu.roll(taken, shift, 1) if shift else taken
                pieces[j] = jnp.where(lane4 == u, moved, pieces[j])
        for j in range(8):
            amp_out[j] = pieces[j]
    if not second:
        cells_out[...] = cells[...].astype(BF16)
        low_out[...] = result[:, 0:3].astype(BF16)
        high_out[...] = result[:, stations - 3 : stations].astype(BF16)

    def drain(p, carry):
        out_copy(p).wait()
        return carry

    lax.fori_loop(0, pairs, drain, 0)


def section(
    state,
    halos,
    fields,
    mixing,
    table,
    quantities=(0, 1, 2),
    flow=None,
    te_local=None,
    band_table=None,
    onto=None,
):
    total, stations, normal, _ = state.shape
    count = len(quantities)
    second, profile, carried = flow is not None, te_local is not None, onto is not None
    pairs = stations // 2
    hbm = pl.BlockSpec(memory_space=pltpu.HBM)
    vmem = pl.BlockSpec(memory_space=pltpu.VMEM)
    smem = pl.BlockSpec(memory_space=pltpu.SMEM)
    args = [state, *halos, *fields, mixing, table]
    specs = [vmem if second else hbm] + [hbm] * 7 + [smem, vmem]
    shapes = [jax.ShapeDtypeStruct(state.shape, F32)]
    aliases = {}
    if second:
        args.append(flow)
        specs.append(hbm)
    if profile:
        args += [te_local, band_table]
        specs += [smem, vmem]
        shapes.append(jax.ShapeDtypeStruct((8, 4, LANES), F32))
    if carried:
        aliases = {len(args): 0}
        args.append(onto)
        specs.append(hbm)
    if not second:
        shapes += [jax.ShapeDtypeStruct((count, 3, normal, LANES), BF16)] * 2
        shapes.append(jax.ShapeDtypeStruct((count, stations // 16, normal, LANES), BF16))
    args = [
        pltpu.with_memory_space_constraint(x, pltpu.HBM) if spec is hbm else x
        for x, spec in zip(args, specs)
    ]
    field = pltpu.VMEM((stations, normal, LANES), BF16)
    block = pltpu.VMEM((count, stations, normal, LANES), F32)
    differences = pltpu.VMEM((count * 2 * normal, 2 * LANES), F32)
    edge = pltpu.VMEM((count, stations // 16, normal, LANES), F32)
    scratch = [
        pltpu.VMEM((count, stations + 6, normal + 16, LANES), F32),
        block,
        differences,
        differences,
        edge,
        edge,
        field,
        field,
        field,
        pltpu.SemaphoreType.DMA((4, 8)),
        pltpu.SemaphoreType.DMA((pairs,)),
    ]
    if second:
        scratch += [block, pltpu.SemaphoreType.DMA((8,))]
    if profile:
        scratch += [pltpu.VMEM((normal, LANES), F32), pltpu.VMEM((stations, LANES), F32)]
    scratch += [pltpu.VMEM((total, 3, normal, LANES), BF16)] * 2
    scratch += [pltpu.VMEM((total, stations // 16, normal, LANES), BF16)] * 2
    scratch.append(pltpu.SemaphoreType.DMA((4,)))
    return pl.pallas_call(
        functools.partial(
            section_kernel,
            second=second,
            profile=profile,
            carried=carried,
            quantities=quantities,
        ),
        out_shape=tuple(shapes),
        in_specs=specs,
        out_specs=tuple([hbm] + [vmem] * (len(shapes) - 1)),
        scratch_shapes=scratch,
        input_output_aliases=aliases,
        compiler_params=pltpu.CompilerParams(vmem_limit_bytes=20 << 20),
        cost_estimate=pl.CostEstimate(
            flops=20000000 * count, transcendentals=0, bytes_accessed=8000000 * count
        ),
        name=("section_two_" if second else "section_one_") + "".join(map(str, quantities)),
    )(*args)


def spectra_kernel(spectra_ref, wanted_ref, own_ref, send_ref):
    stations, bands, slots = spectra_ref.shape
    width = own_ref.shape[1]
    segs = wanted_ref.shape[0]
    lanes = lax.broadcasted_iota(jnp.int32, (1, width), 1)
    wanted = jnp.zeros((1, width), jnp.int32)
    for k in range(segs):
        wanted = jnp.where(lax.rem(lanes, segs) == k, wanted_ref[k], wanted)
    wanted = wanted + (slots // 2) * lax.rem(lax.div(lanes, segs), 2)
    rows = spectra_ref[...].astype(F32).reshape(stations * bands, slots).astype(BF16)
    slot = lax.broadcasted_iota(jnp.int32, (slots, width), 0)
    choose = jnp.where(slot == wanted, 1.0, 0.0).astype(BF16)
    got = jnp.dot(rows, choose, preferred_element_type=F32)
    row_band = lax.rem(lax.broadcasted_iota(jnp.int32, got.shape, 0), bands)
    lane_band = lax.div(lax.broadcasted_iota(jnp.int32, got.shape, 1), width // bands)
    got = jnp.where(row_band == lane_band, got, 0.0).reshape(stations, bands, width)
    packed = jnp.sum(got, axis=1).astype(BF16)
    own_ref[...] = packed
    for d in range(send_ref.shape[0]):
        send_ref[d] = packed


def stored_kernel(prior_ref, every_ref, own_ref, ramp_ref, out_ref, left):
    bands, stations, tile = prior_ref.shape[1:]
    width = own_ref.shape[1]

    @pl.when(pl.program_id(0) == 0)
    def _():
        own = own_ref[...].astype(F32)
        lane = lax.broadcasted_iota(jnp.int32, own.shape, 1)
        real = lax.rem(lane, 32) < 16
        turned = jnp.where(real, pltpu.roll(own, width - 16, 1), -pltpu.roll(own, 16, 1))
        for c, part in enumerate((own, turned)):
            part = part * ramp_ref[...]
            high = part.astype(BF16).astype(F32)
            low = part - high
            for b in range(bands):
                at = (c * bands + b) * stations
                keep = lax.div(lane, 32) == b
                rows = slice(at, at + stations)
                left[rows, 0:width] = jnp.where(keep, high, 0.0).astype(BF16)
                left[rows, width : 2 * width] = jnp.where(keep, low, 0.0).astype(BF16)

    stored = every_ref[...]
    got = nt_dot(left[...], jnp.concatenate([stored, stored], axis=1))
    out_ref[...] = DECAY * prior_ref[...] + got.reshape(2, bands, stations, tile)


def amplitude_kernel(known_ref, amp_ref, where_ref, rep_ref, out_ref, left):
    step = pl.program_id(0)
    bands, stations, tile = known_ref.shape[1:]
    blocks = tile // stations
    sources = amp_ref.shape[0] // blocks // pl.num_programs(0)

    def spread(source):
        whole = amp_ref[pl.ds(source * sources, sources)].astype(F32)
        total = whole[0]
        for j in range(1, sources):
            total = total + whole[j]
        lane = lax.div(lax.broadcasted_iota(jnp.int32, (8, LANES), 1), 16)
        here = lane == lax.broadcasted_iota(jnp.int32, (8, LANES), 0)
        rows = [
            jnp.where(here, jnp.broadcast_to(total[t : t + 1, :], (8, LANES)), 0.0)
            for t in range(4)
        ]
        return jnp.concatenate(rows).astype(BF16)

    @pl.when(step == 0)
    def _():
        mine = spread(where_ref[0])
        place = lax.rem(lax.broadcasted_iota(jnp.int32, (stations, LANES), 1), 8)
        for c in range(2):
            amp = jnp.dot(mine, rep_ref[c], preferred_element_type=F32)
            for b in range(bands):
                at = (c * bands + b) * stations
                left[at : at + stations, :] = jnp.where(place == b, amp, 0.0).astype(BF16)

    right = jnp.concatenate([spread(step * blocks + i) for i in range(blocks)])
    got = nt_dot(left[...], right)
    out_ref[...] = known_ref[...] + got.reshape(2, bands, stations, tile)


def amplitude_tables():
    index = np.arange(LANES)
    same = (index[:, None] % 16 == index[None, :] % 16).astype(np.float32)
    other = (index[:, None] % 8 == index[None, :] % 8) & (
        (index[:, None] % 16) // 8 != (index[None, :] % 16) // 8
    )
    sign = np.where((index % 16) // 8 == 0, 1.0, -1.0)
    return np.stack([same, other * sign[None, :]]).astype(ml_dtypes.bfloat16)


def shards(
    flow_state,
    vel_span,
    vel_chord,
    viscosity,
    mixing,
    te_index,
    band_response,
    spectra,
    offsets,
    prior_gram_blocks,
):
    count, stations, normal, cells = flow_state.shape
    bands, slots = spectra.shape[1], spectra.shape[2] // 2
    segs = offsets.shape[0]
    span_n, chord_n = lax.axis_size("span"), lax.axis_size("chord")
    span_pos, chord_pos = lax.axis_index("span"), lax.axis_index("chord")
    table = chord_matrices()
    fields = (vel_span, vel_chord, viscosity)

    def exchange(low, high, edge):
        up = [(i, (i + 1) % span_n) for i in range(span_n)]
        down = [(b, a) for a, b in up]
        forward = [(i, i + 1) for i in range(chord_n - 1)]
        backward = [(b, a) for a, b in forward]
        return (
            lax.ppermute(high, "span", up),
            lax.ppermute(low, "span", down),
            lax.ppermute(edge, "chord", forward),
            lax.ppermute(edge, "chord", backward),
        )

    edge_shape = jax.ShapeDtypeStruct((count, stations // 16, normal, LANES), BF16)
    ends_shape = jax.ShapeDtypeStruct((count, 3, normal, LANES), BF16)

    def per_quantity(shape):
        return pl.BlockSpec((1,) + shape.shape[1:], lambda q: (q, 0, 0, 0))

    edge, low, high = pl.pallas_call(
        edges_kernel,
        grid=(count,),
        out_shape=(edge_shape, ends_shape, ends_shape),
        in_specs=[per_quantity(flow_state)],
        out_specs=(per_quantity(edge_shape), per_quantity(ends_shape), per_quantity(ends_shape)),
        name="edges",
    )(flow_state)
    halos = exchange(low, high, edge)

    width = bands * 2 * segs
    _, stored = lax.optimization_barrier((edge, spectra))
    packed, send = pl.pallas_call(
        spectra_kernel,
        out_shape=(
            jax.ShapeDtypeStruct((stations, width), BF16),
            jax.ShapeDtypeStruct((span_n, stations, width), BF16),
        ),
        in_specs=[
            pl.BlockSpec(memory_space=pltpu.VMEM),
            pl.BlockSpec(memory_space=pltpu.SMEM),
        ],
        name="spectra",
    )(stored, offsets)
    every = lax.all_to_all(send, "span", 0, 0, tiled=True).reshape(span_n * stations, width)

    (section_one, low, high, edge) = section(flow_state, halos, fields, mixing, table)
    halos = exchange(low, high, edge)

    te_local = te_index - chord_pos * cells
    band_table = band_response.reshape(normal, 2, chord_n, bands).transpose(0, 2, 1, 3)
    band_table = band_table.reshape(normal, chord_n * 2 * bands)
    flow_next, amps = section(
        section_one,
        halos,
        fields,
        mixing,
        table,
        (0,),
        flow=flow_state,
        te_local=te_local,
        band_table=band_table,
    )
    amps = jnp.broadcast_to(amps.astype(BF16)[None], (span_n,) + amps.shape)
    amps = lax.all_to_all(
        amps.reshape((span_n * chord_n,) + amps.shape[2:]), ("span", "chord"), 0, 0, tiled=True
    )
    (flow_next,) = section(
        section_one, halos, fields, mixing, table, (1, 2), flow=flow_state, onto=flow_next
    )

    ramp = np.tile((np.arange(segs, dtype=np.float32) + 1) / segs, 2 * bands)[None]
    tiles = 4
    tile = span_n * stations // tiles
    gram_shape = jax.ShapeDtypeStruct(prior_gram_blocks.shape, F32)
    gram_block = pl.BlockSpec((2, bands, stations, tile), lambda t: (0, 0, 0, t))
    params = pltpu.CompilerParams(vmem_limit_bytes=24 << 20)

    def whole(x):
        return pl.BlockSpec(x.shape, lambda t: (0,) * x.ndim)

    known = pl.pallas_call(
        stored_kernel,
        grid=(tiles,),
        out_shape=gram_shape,
        in_specs=[
            gram_block,
            pl.BlockSpec((tile, width), lambda t: (t, 0)),
            whole(packed),
            whole(ramp),
        ],
        out_specs=gram_block,
        scratch_shapes=[pltpu.VMEM((2 * bands * stations, 2 * width), BF16)],
        compiler_params=params,
        cost_estimate=pl.CostEstimate(
            flops=30000000, transcendentals=0, bytes_accessed=12000000
        ),
        name="gram_stored",
    )(
        pltpu.with_memory_space_constraint(prior_gram_blocks, pltpu.HBM),
        pltpu.with_memory_space_constraint(every, pltpu.HBM),
        packed,
        ramp,
    )
    known, flow_next = lax.optimization_barrier((known, flow_next))
    reps = amplitude_tables()
    gram_next = pl.pallas_call(
        amplitude_kernel,
        grid=(tiles,),
        out_shape=gram_shape,
        in_specs=[
            gram_block,
            whole(amps),
            pl.BlockSpec(memory_space=pltpu.SMEM),
            whole(reps),
        ],
        out_specs=gram_block,
        scratch_shapes=[pltpu.VMEM((2 * bands * stations, LANES), BF16)],
        compiler_params=params,
        name="gram_amplitudes",
    )(
        known,
        amps,
        span_pos.reshape(1),
        reps,
    )
    return (flow_next, gram_next)


def solution(mesh):
    return jax.shard_map(
        shards,
        mesh=mesh,
        in_specs=(
            P(None, "span", None, "chord"),
            P("span", None, "chord"),
            P("span", None, "chord"),
            P("span", None, "chord"),
            P(),
            P("span"),
            P(),
            P("span", "chord", None),
            P(),
            P(None, "chord", "span", None),
        ),
        out_specs=(P(None, "span", None, "chord"), P(None, "chord", "span", None)),
        check_vma=False,
    )
```

```python
import functools

import jax
import jax.numpy as jnp
import ml_dtypes
import numpy as np
from jax import lax
from jax.experimental import pallas as pl
from jax.experimental.pallas import tpu as pltpu
from jax.sharding import PartitionSpec as P

FIRST = (45, -9, 1)
SECOND = (270, -27, 2)
CENTRE = -490
TIME_STEP = 0.6
DECAY = 0.9
F32 = jnp.float32
BF16 = jnp.bfloat16
LANES = 128


def chord_matrices():
    inner = np.zeros((LANES, 2 * LANES), np.float32)
    outer = np.zeros((LANES, 2 * LANES), np.float32)

    def row(cell):
        if cell < 0:
            return outer, cell + 3
        if cell >= LANES:
            return outer, cell - LANES + 3
        return inner, cell

    for cell in range(LANES):
        inner[cell, LANES + cell] += CENTRE
        for reach in (1, 2, 3):
            for sign in (1, -1):
                table, index = row(cell + sign * reach)
                table[index, cell] += sign * FIRST[reach - 1]
                table[index, LANES + cell] += SECOND[reach - 1]
    return np.concatenate([inner, inner, outer]).astype(ml_dtypes.bfloat16)


def nt_dot(a, b):
    return lax.dot_general(a, b, (((1,), (1,)), ((), ())), preferred_element_type=F32)


def fine_dot(a, b):
    def pieces(x):
        one = x.astype(BF16)
        x = x - one.astype(F32)
        two = x.astype(BF16)
        return one, two, (x - two.astype(F32)).astype(BF16)

    left, right = pieces(a), pieces(b)
    total = None
    for i, j in ((2, 0), (0, 2), (1, 1), (1, 0), (0, 1), (0, 0)):
        part = jnp.dot(left[i], right[j], preferred_element_type=F32)
        total = part if total is None else total + part
    return total


def edge_lanes(shape):
    return lax.div(lax.broadcasted_iota(jnp.int32, shape, len(shape) - 1), 8)


def edges_kernel(flow_ref, cells_ref, low_ref, high_ref):
    stations, normal = flow_ref.shape[1:3]
    lane = edge_lanes((16, LANES))
    for half in range(stations // 16):
        for tile in range(normal // 16):
            rows = slice(16 * tile, 16 * tile + 16)
            packed = jnp.zeros((16, LANES), F32)
            for s in range(16):
                moved = pltpu.roll(flow_ref[0, 16 * half + s, rows, :], (3 + 8 * s) % LANES, 1)
                packed = jnp.where(lane == s, moved, packed)
            cells_ref[0, half, rows, :] = packed.astype(BF16)
    low_ref[0] = flow_ref[0, 0:3].astype(BF16)
    high_ref[0] = flow_ref[0, stations - 3 : stations].astype(BF16)


def section_kernel(*refs, second, profile, carried, quantities):
    refs = list(refs)
    take = refs.pop
    state_ref = take(0)
    halo_hbm = [take(0) for _ in range(4)]
    vs_hbm, vc_hbm, nu_hbm = (take(0) for _ in range(3))
    mix, table_ref = take(0), take(0)
    if second:
        flow_hbm = take(0)
    if profile:
        te_ref, band_ref = take(0), take(0)
    if carried:
        take(0)
    out_hbm = take(0)
    if profile:
        amp_out = take(0)
    if not second:
        low_out, high_out, cells_out = (take(0) for _ in range(3))
    wide, result, chord_a, chord_b, halos, cells, vs, vc, nu, in_sem, out_sem = (take(0) for _ in range(11))
    if second:
        before, before_sem = take(0), take(0)
    if profile:
        columns, amps = take(0), take(0)
    span_low, span_high, chord_low, chord_high, halo_sem = (take(0) for _ in range(5))

    count, stations, normal = len(quantities), vs.shape[0], vs.shape[1]
    everything = range(state_ref.shape[0])
    some = pl.ds(quantities[0], count)
    chunks, pairs = 8, stations // 2
    per = stations // chunks

    def copies(c):
        rows = pl.ds(per * c, per)
        todo = [
            pltpu.make_async_copy(
                state_ref.at[some, rows],
                wide.at[:, pl.ds(3 + per * c, per), pl.ds(8, normal), :],
                in_sem.at[0, c],
            ),
            pltpu.make_async_copy(vs_hbm.at[rows], vs.at[rows], in_sem.at[1, c]),
            pltpu.make_async_copy(vc_hbm.at[rows], vc.at[rows], in_sem.at[2, c]),
            pltpu.make_async_copy(nu_hbm.at[rows], nu.at[rows], in_sem.at[3, c]),
        ]
        if second:
            todo.append(
                pltpu.make_async_copy(flow_hbm.at[some, rows], before.at[:, rows], before_sem.at[c])
            )
        return todo

    halo_copies = [
        pltpu.make_async_copy(source, target, halo_sem.at[i])
        for i, (source, target) in enumerate(
            zip(halo_hbm, (span_low, span_high, chord_low, chord_high))
        )
    ]
    for copy in halo_copies:
        copy.start()
    for c in range(chunks):
        for copy in copies(c):
            copy.start()

    nothing = jnp.zeros((count, stations, 8, LANES), F32)
    wide[:, 3 : 3 + stations, 0:8, :] = nothing
    wide[:, 3 : 3 + stations, 8 + normal : 16 + normal, :] = nothing
    if profile:
        columns[...] = jnp.zeros(columns.shape, F32)
    for copy in halo_copies:
        copy.wait()
    wide[:, 0:3, 8 : 8 + normal, :] = span_low[some].astype(F32)
    wide[:, 3 + stations : 6 + stations, 8 : 8 + normal, :] = span_high[some].astype(F32)
    place = lax.rem(lax.broadcasted_iota(jnp.int32, (normal, LANES), 1), 8)
    for local, q in enumerate(quantities):
        for half in range(stations // 16):
            near = jnp.where(
                place < 3, chord_low[q, half].astype(F32), chord_high[q, half].astype(F32)
            )
            halos[local, half] = jnp.where(place < 6, near, 0.0)

    def matmuls(p, chord):
        half = lax.div(p, 8)
        parts = []
        for q in range(count):
            for d in range(2):
                slab = wide[q, 3 + 2 * p + d, 8 : 8 + normal, :]
                high = slab.astype(BF16)
                low = (slab - high.astype(F32)).astype(BF16)
                shift = lax.rem(LANES - 8 * lax.rem(2 * p + d, 16), LANES)
                beyond = pltpu.roll(halos[q, half], shift, 1).astype(BF16)
                parts.append(jnp.concatenate([high, low, beyond], axis=1))
        chord[...] = jnp.dot(
            jnp.concatenate(parts), table_ref[...], preferred_element_type=F32
        )

    scale = 0.5 if second else 1.0
    couple = [
        [scale * ((1.0 if q == e else 0.0) + TIME_STEP * mix[q, e]) for e in everything]
        for q in quantities
    ]
    ROWS = 16
    lane = lax.broadcasted_iota(jnp.int32, (ROWS, LANES), 1)

    def body(i, carry):
        pair(2 * i, chord_a, chord_b)
        pair(2 * i + 1, chord_b, chord_a)
        return carry

    def pair(p, chord, later):
        matmuls(jnp.minimum(p + 1, pairs - 1), later)
        for half in range(2):
            s = 2 * p + half
            for tile in range(normal // ROWS):
                rows = slice(ROWS * tile, ROWS * tile + ROWS)
                a = vs[s, rows, :].astype(F32) * (-scale * TIME_STEP / 60)
                b = vc[s, rows, :].astype(F32) * (-scale * TIME_STEP / 60)
                g = nu[s, rows, :].astype(F32) * (scale * TIME_STEP / 180)
                centre = [
                    wide[e - quantities[0], 3 + s, 8 + ROWS * tile : 8 + ROWS * tile + ROWS, :]
                    if e in quantities
                    else state_ref[e, s, rows, :]
                    for e in everything
                ]
                for local, q in enumerate(quantities):

                    def at(ds, dn):
                        low = 8 + ROWS * tile + dn
                        return wide[local, 3 + s + ds, low : low + ROWS, :]

                    first = None
                    both = None
                    for reach in (1, 2, 3):
                        up, down = at(reach, 0), at(-reach, 0)
                        diff = up - down
                        total = (up + down) + (at(0, reach) + at(0, -reach))
                        if FIRST[reach - 1] != 1:
                            diff = diff * float(FIRST[reach - 1])
                        total = total * float(SECOND[reach - 1])
                        first = diff if first is None else first + diff
                        both = total if both is None else both + total
                    start = (2 * local + half) * normal + ROWS * tile
                    crow = slice(start, start + ROWS)
                    chord_first = chord[crow, 0:LANES]
                    chord_second = chord[crow, LANES : 2 * LANES]
                    both = both + (centre[q] * float(2 * CENTRE) + chord_second)
                    value = a * first + b * chord_first + g * both
                    for e in everything:
                        value = value + couple[local][e] * centre[e]
                    if second:
                        value = value + 0.5 * before[local, s, rows, :]
                    result[local, s, rows, :] = value
                    if profile and q == 0:
                        hit = jnp.where(lane == te_ref[s], value, 0.0)
                        column = jnp.sum(hit, axis=1, keepdims=True)
                        columns[rows, :] += jnp.where(lane == s, column, 0.0)
                    if not second:
                        station = lax.rem(s, 16)
                        moved = pltpu.roll(value, lax.rem(3 + 8 * station, LANES), 1)
                        kept = cells[q, lax.div(p, 8), rows, :]
                        cells[q, lax.div(p, 8), rows, :] = jnp.where(
                            lax.div(lane, 8) == station, moved, kept
                        )
        out_copy(p).start()

    def out_copy(p):
        two = pl.ds(2 * p, 2)
        return pltpu.make_async_copy(result.at[:, two], out_hbm.at[some, two], out_sem.at[p])

    def arrive(c):
        for copy in copies(c):
            copy.wait()

    arrive(0)
    matmuls(0, chord_a)
    for c in range(chunks):
        if c + 1 < chunks:
            arrive(c + 1)
        lax.fori_loop(c * pairs // chunks // 2, (c + 1) * pairs // chunks // 2, body, 0)

    if profile:
        amp = fine_dot(columns[...].T, band_ref[...])
        amps[...] = amp[:stations].astype(BF16).astype(F32)
        lane4 = lax.div(lax.broadcasted_iota(jnp.int32, (4, LANES), 1), 16)
        pieces = [jnp.zeros((4, LANES), F32) for _ in range(8)]
        for u in range(8):
            taken = amps[pl.ds(u, 4, stride=8), :]
            for j in range(8):
                shift = (16 * (u - j)) % LANES
                moved = pltpu.roll(taken, shift, 1) if shift else taken
                pieces[j] = jnp.where(lane4 == u, moved, pieces[j])
        for j in range(8):
            amp_out[j] = pieces[j]
    if not second:
        cells_out[...] = cells[...].astype(BF16)
        low_out[...] = result[:, 0:3].astype(BF16)
        high_out[...] = result[:, stations - 3 : stations].astype(BF16)

    def drain(p, carry):
        out_copy(p).wait()
        return carry

    lax.fori_loop(0, pairs, drain, 0)


def section(
    state,
    halos,
    fields,
    mixing,
    table,
    quantities=(0, 1, 2),
    flow=None,
    te_local=None,
    band_table=None,
    onto=None,
):
    total, stations, normal, _ = state.shape
    count = len(quantities)
    second, profile, carried = flow is not None, te_local is not None, onto is not None
    pairs = stations // 2
    hbm = pl.BlockSpec(memory_space=pltpu.HBM)
    vmem = pl.BlockSpec(memory_space=pltpu.VMEM)
    smem = pl.BlockSpec(memory_space=pltpu.SMEM)
    args = [state, *halos, *fields, mixing, table]
    specs = [vmem if second else hbm] + [hbm] * 7 + [smem, vmem]
    shapes = [jax.ShapeDtypeStruct(state.shape, F32)]
    aliases = {}
    if second:
        args.append(flow)
        specs.append(hbm)
    if profile:
        args += [te_local, band_table]
        specs += [smem, vmem]
        shapes.append(jax.ShapeDtypeStruct((8, 4, LANES), F32))
    if carried:
        aliases = {len(args): 0}
        args.append(onto)
        specs.append(hbm)
    if not second:
        shapes += [jax.ShapeDtypeStruct((count, 3, normal, LANES), BF16)] * 2
        shapes.append(jax.ShapeDtypeStruct((count, stations // 16, normal, LANES), BF16))
    args = [
        pltpu.with_memory_space_constraint(x, pltpu.HBM) if spec is hbm else x
        for x, spec in zip(args, specs)
    ]
    field = pltpu.VMEM((stations, normal, LANES), BF16)
    block = pltpu.VMEM((count, stations, normal, LANES), F32)
    differences = pltpu.VMEM((count * 2 * normal, 2 * LANES), F32)
    edge = pltpu.VMEM((count, stations // 16, normal, LANES), F32)
    scratch = [
        pltpu.VMEM((count, stations + 6, normal + 16, LANES), F32),
        block,
        differences,
        differences,
        edge,
        edge,
        field,
        field,
        field,
        pltpu.SemaphoreType.DMA((4, 8)),
        pltpu.SemaphoreType.DMA((pairs,)),
    ]
    if second:
        scratch += [block, pltpu.SemaphoreType.DMA((8,))]
    if profile:
        scratch += [pltpu.VMEM((normal, LANES), F32), pltpu.VMEM((stations, LANES), F32)]
    scratch += [pltpu.VMEM((total, 3, normal, LANES), BF16)] * 2
    scratch += [pltpu.VMEM((total, stations // 16, normal, LANES), BF16)] * 2
    scratch.append(pltpu.SemaphoreType.DMA((4,)))
    return pl.pallas_call(
        functools.partial(
            section_kernel,
            second=second,
            profile=profile,
            carried=carried,
            quantities=quantities,
        ),
        out_shape=tuple(shapes),
        in_specs=specs,
        out_specs=tuple([hbm] + [vmem] * (len(shapes) - 1)),
        scratch_shapes=scratch,
        input_output_aliases=aliases,
        compiler_params=pltpu.CompilerParams(vmem_limit_bytes=20 << 20),
        cost_estimate=pl.CostEstimate(
            flops=20000000 * count, transcendentals=0, bytes_accessed=8000000 * count
        ),
        name=("section_two_" if second else "section_one_") + "".join(map(str, quantities)),
    )(*args)


def spectra_kernel(spectra_ref, wanted_ref, own_ref, send_ref):
    stations, bands, slots = spectra_ref.shape
    width = own_ref.shape[1]
    segs = wanted_ref.shape[0]
    lanes = lax.broadcasted_iota(jnp.int32, (1, width), 1)
    wanted = jnp.zeros((1, width), jnp.int32)
    for k in range(segs):
        wanted = jnp.where(lax.rem(lanes, segs) == k, wanted_ref[k], wanted)
    wanted = wanted + (slots // 2) * lax.rem(lax.div(lanes, segs), 2)
    rows = spectra_ref[...].astype(F32).reshape(stations * bands, slots).astype(BF16)
    slot = lax.broadcasted_iota(jnp.int32, (slots, width), 0)
    choose = jnp.where(slot == wanted, 1.0, 0.0).astype(BF16)
    got = jnp.dot(rows, choose, preferred_element_type=F32)
    row_band = lax.rem(lax.broadcasted_iota(jnp.int32, got.shape, 0), bands)
    lane_band = lax.div(lax.broadcasted_iota(jnp.int32, got.shape, 1), width // bands)
    got = jnp.where(row_band == lane_band, got, 0.0).reshape(stations, bands, width)
    packed = jnp.sum(got, axis=1).astype(BF16)
    own_ref[...] = packed
    for d in range(send_ref.shape[0]):
        send_ref[d] = packed


def stored_kernel(prior_ref, every_ref, own_ref, ramp_ref, out_ref, left):
    bands, stations, tile = prior_ref.shape[1:]
    width = own_ref.shape[1]

    @pl.when(pl.program_id(0) == 0)
    def _():
        own = own_ref[...].astype(F32)
        lane = lax.broadcasted_iota(jnp.int32, own.shape, 1)
        real = lax.rem(lane, 32) < 16
        turned = jnp.where(real, pltpu.roll(own, width - 16, 1), -pltpu.roll(own, 16, 1))
        for c, part in enumerate((own, turned)):
            part = part * ramp_ref[...]
            high = part.astype(BF16).astype(F32)
            low = part - high
            for b in range(bands):
                at = (c * bands + b) * stations
                keep = lax.div(lane, 32) == b
                rows = slice(at, at + stations)
                left[rows, 0:width] = jnp.where(keep, high, 0.0).astype(BF16)
                left[rows, width : 2 * width] = jnp.where(keep, low, 0.0).astype(BF16)

    stored = every_ref[...]
    got = nt_dot(left[...], jnp.concatenate([stored, stored], axis=1))
    out_ref[...] = DECAY * prior_ref[...] + got.reshape(2, bands, stations, tile)


def amplitude_kernel(known_ref, amp_ref, where_ref, rep_ref, out_ref, left):
    step = pl.program_id(0)
    bands, stations, tile = known_ref.shape[1:]
    blocks = tile // stations
    sources = amp_ref.shape[0] // blocks // pl.num_programs(0)

    def spread(source):
        whole = amp_ref[pl.ds(source * sources, sources)].astype(F32)
        total = whole[0]
        for j in range(1, sources):
            total = total + whole[j]
        lane = lax.div(lax.broadcasted_iota(jnp.int32, (8, LANES), 1), 16)
        here = lane == lax.broadcasted_iota(jnp.int32, (8, LANES), 0)
        rows = [
            jnp.where(here, jnp.broadcast_to(total[t : t + 1, :], (8, LANES)), 0.0)
            for t in range(4)
        ]
        return jnp.concatenate(rows).astype(BF16)

    @pl.when(step == 0)
    def _():
        mine = spread(where_ref[0])
        place = lax.rem(lax.broadcasted_iota(jnp.int32, (stations, LANES), 1), 8)
        for c in range(2):
            amp = jnp.dot(mine, rep_ref[c], preferred_element_type=F32)
            for b in range(bands):
                at = (c * bands + b) * stations
                left[at : at + stations, :] = jnp.where(place == b, amp, 0.0).astype(BF16)

    right = jnp.concatenate([spread(step * blocks + i) for i in range(blocks)])
    got = nt_dot(left[...], right)
    out_ref[...] = known_ref[...] + got.reshape(2, bands, stations, tile)


def amplitude_tables():
    index = np.arange(LANES)
    same = (index[:, None] % 16 == index[None, :] % 16).astype(np.float32)
    other = (index[:, None] % 8 == index[None, :] % 8) & (
        (index[:, None] % 16) // 8 != (index[None, :] % 16) // 8
    )
    sign = np.where((index % 16) // 8 == 0, 1.0, -1.0)
    return np.stack([same, other * sign[None, :]]).astype(ml_dtypes.bfloat16)


def shards(
    flow_state,
    vel_span,
    vel_chord,
    viscosity,
    mixing,
    te_index,
    band_response,
    spectra,
    offsets,
    prior_gram_blocks,
):
    count, stations, normal, cells = flow_state.shape
    bands, slots = spectra.shape[1], spectra.shape[2] // 2
    segs = offsets.shape[0]
    span_n, chord_n = lax.axis_size("span"), lax.axis_size("chord")
    span_pos, chord_pos = lax.axis_index("span"), lax.axis_index("chord")
    table = chord_matrices()
    fields = (vel_span, vel_chord, viscosity)

    def exchange(low, high, edge):
        up = [(i, (i + 1) % span_n) for i in range(span_n)]
        down = [(b, a) for a, b in up]
        forward = [(i, i + 1) for i in range(chord_n - 1)]
        backward = [(b, a) for a, b in forward]
        return (
            lax.ppermute(high, "span", up),
            lax.ppermute(low, "span", down),
            lax.ppermute(edge, "chord", forward),
            lax.ppermute(edge, "chord", backward),
        )

    edge_shape = jax.ShapeDtypeStruct((count, stations // 16, normal, LANES), BF16)
    ends_shape = jax.ShapeDtypeStruct((count, 3, normal, LANES), BF16)

    def per_quantity(shape):
        return pl.BlockSpec((1,) + shape.shape[1:], lambda q: (q, 0, 0, 0))

    edge, low, high = pl.pallas_call(
        edges_kernel,
        grid=(count,),
        out_shape=(edge_shape, ends_shape, ends_shape),
        in_specs=[per_quantity(flow_state)],
        out_specs=(per_quantity(edge_shape), per_quantity(ends_shape), per_quantity(ends_shape)),
        name="edges",
    )(flow_state)
    halos = exchange(low, high, edge)

    width = bands * 2 * segs
    _, stored = lax.optimization_barrier((edge, spectra))
    packed, send = pl.pallas_call(
        spectra_kernel,
        out_shape=(
            jax.ShapeDtypeStruct((stations, width), BF16),
            jax.ShapeDtypeStruct((span_n, stations, width), BF16),
        ),
        in_specs=[
            pl.BlockSpec(memory_space=pltpu.VMEM),
            pl.BlockSpec(memory_space=pltpu.SMEM),
        ],
        name="spectra",
    )(stored, offsets)
    every = lax.all_to_all(send, "span", 0, 0, tiled=True).reshape(span_n * stations, width)

    (section_one, low, high, edge) = section(flow_state, halos, fields, mixing, table)
    halos = exchange(low, high, edge)

    ramp = np.tile((np.arange(segs, dtype=np.float32) + 1) / segs, 2 * bands)[None]
    tiles = 4
    tile = span_n * stations // tiles
    gram_shape = jax.ShapeDtypeStruct(prior_gram_blocks.shape, F32)
    gram_block = pl.BlockSpec((2, bands, stations, tile), lambda t: (0, 0, 0, t))
    params = pltpu.CompilerParams(vmem_limit_bytes=24 << 20)

    def whole(x):
        return pl.BlockSpec(x.shape, lambda t: (0,) * x.ndim)

    known = pl.pallas_call(
        stored_kernel,
        grid=(tiles,),
        out_shape=gram_shape,
        in_specs=[
            gram_block,
            pl.BlockSpec((tile, width), lambda t: (t, 0)),
            whole(packed),
            whole(ramp),
        ],
        out_specs=gram_block,
        scratch_shapes=[pltpu.VMEM((2 * bands * stations, 2 * width), BF16)],
        compiler_params=params,
        cost_estimate=pl.CostEstimate(
            flops=30000000, transcendentals=0, bytes_accessed=12000000
        ),
        name="gram_stored",
    )(
        pltpu.with_memory_space_constraint(prior_gram_blocks, pltpu.HBM),
        pltpu.with_memory_space_constraint(every, pltpu.HBM),
        packed,
        ramp,
    )
    halos, known = lax.optimization_barrier((halos, known))

    te_local = te_index - chord_pos * cells
    band_table = band_response.reshape(normal, 2, chord_n, bands).transpose(0, 2, 1, 3)
    band_table = band_table.reshape(normal, chord_n * 2 * bands)
    flow_next, amps = section(
        section_one,
        halos,
        fields,
        mixing,
        table,
        (0,),
        flow=flow_state,
        te_local=te_local,
        band_table=band_table,
    )
    amps = jnp.broadcast_to(amps.astype(BF16)[None], (span_n,) + amps.shape)
    amps = lax.all_to_all(
        amps.reshape((span_n * chord_n,) + amps.shape[2:]), ("span", "chord"), 0, 0, tiled=True
    )
    (flow_next,) = section(
        section_one, halos, fields, mixing, table, (1, 2), flow=flow_state, onto=flow_next
    )

    known, flow_next = lax.optimization_barrier((known, flow_next))
    reps = amplitude_tables()
    gram_next = pl.pallas_call(
        amplitude_kernel,
        grid=(tiles,),
        out_shape=gram_shape,
        in_specs=[
            gram_block,
            whole(amps),
            pl.BlockSpec(memory_space=pltpu.SMEM),
            whole(reps),
        ],
        out_specs=gram_block,
        scratch_shapes=[pltpu.VMEM((2 * bands * stations, LANES), BF16)],
        compiler_params=params,
        name="gram_amplitudes",
    )(
        known,
        amps,
        span_pos.reshape(1),
        reps,
    )
    return (flow_next, gram_next)


def solution(mesh):
    return jax.shard_map(
        shards,
        mesh=mesh,
        in_specs=(
            P(None, "span", None, "chord"),
            P("span", None, "chord"),
            P("span", None, "chord"),
            P("span", None, "chord"),
            P(),
            P("span"),
            P(),
            P("span", "chord", None),
            P(),
            P(None, "chord", "span", None),
        ),
        out_specs=(P(None, "span", None, "chord"), P(None, "chord", "span", None)),
        check_vma=False,
    )
```

```python
import functools

import jax
import jax.numpy as jnp
import ml_dtypes
import numpy as np
from jax import lax
from jax.experimental import pallas as pl
from jax.experimental.pallas import tpu as pltpu
from jax.sharding import PartitionSpec as P

FIRST = (45, -9, 1)
SECOND = (270, -27, 2)
CENTRE = -490
TIME_STEP = 0.6
DECAY = 0.9
F32 = jnp.float32
BF16 = jnp.bfloat16
LANES = 128


def chord_matrices():
    inner = np.zeros((LANES, 2 * LANES), np.float32)
    outer = np.zeros((LANES, 2 * LANES), np.float32)

    def row(cell):
        if cell < 0:
            return outer, cell + 3
        if cell >= LANES:
            return outer, cell - LANES + 3
        return inner, cell

    for cell in range(LANES):
        inner[cell, LANES + cell] += CENTRE
        for reach in (1, 2, 3):
            for sign in (1, -1):
                table, index = row(cell + sign * reach)
                table[index, cell] += sign * FIRST[reach - 1]
                table[index, LANES + cell] += SECOND[reach - 1]
    return np.concatenate([inner, inner, outer]).astype(ml_dtypes.bfloat16)


def nt_dot(a, b):
    return lax.dot_general(a, b, (((1,), (1,)), ((), ())), preferred_element_type=F32)


def fine_dot(a, b):
    def pieces(x):
        one = x.astype(BF16)
        x = x - one.astype(F32)
        two = x.astype(BF16)
        return one, two, (x - two.astype(F32)).astype(BF16)

    left, right = pieces(a), pieces(b)
    total = None
    for i, j in ((2, 0), (0, 2), (1, 1), (1, 0), (0, 1), (0, 0)):
        part = jnp.dot(left[i], right[j], preferred_element_type=F32)
        total = part if total is None else total + part
    return total


def edge_lanes(shape):
    return lax.div(lax.broadcasted_iota(jnp.int32, shape, len(shape) - 1), 8)


def edges_kernel(flow_ref, cells_ref, low_ref, high_ref):
    stations, normal = flow_ref.shape[1:3]
    lane = edge_lanes((16, LANES))
    for half in range(stations // 16):
        for tile in range(normal // 16):
            rows = slice(16 * tile, 16 * tile + 16)
            packed = jnp.zeros((16, LANES), F32)
            for s in range(16):
                moved = pltpu.roll(flow_ref[0, 16 * half + s, rows, :], (3 + 8 * s) % LANES, 1)
                packed = jnp.where(lane == s, moved, packed)
            cells_ref[0, half, rows, :] = packed.astype(BF16)
    low_ref[0] = flow_ref[0, 0:3].astype(BF16)
    high_ref[0] = flow_ref[0, stations - 3 : stations].astype(BF16)


def section_kernel(*refs, second, profile, carried, quantities):
    refs = list(refs)
    take = refs.pop
    state_ref = take(0)
    halo_hbm = [take(0) for _ in range(4)]
    vs_hbm, vc_hbm, nu_hbm = (take(0) for _ in range(3))
    mix, table_ref = take(0), take(0)
    if second:
        flow_hbm = take(0)
    if profile:
        te_ref, band_ref = take(0), take(0)
    if carried:
        take(0)
    out_hbm = take(0)
    if profile:
        amp_out = take(0)
    if not second:
        low_out, high_out, cells_out = (take(0) for _ in range(3))
    wide, result, chord_a, chord_b, halos, cells, vs, vc, nu, in_sem, out_sem = (take(0) for _ in range(11))
    if second:
        before, before_sem = take(0), take(0)
    if profile:
        columns, amps = take(0), take(0)
    span_low, span_high, chord_low, chord_high, halo_sem = (take(0) for _ in range(5))

    count, stations, normal = len(quantities), vs.shape[0], vs.shape[1]
    everything = range(state_ref.shape[0])
    some = pl.ds(quantities[0], count)
    chunks, pairs = 8, stations // 2
    per = stations // chunks

    def copies(c):
        rows = pl.ds(per * c, per)
        todo = [
            pltpu.make_async_copy(
                state_ref.at[some, rows],
                wide.at[:, pl.ds(3 + per * c, per), pl.ds(8, normal), :],
                in_sem.at[0, c],
            ),
            pltpu.make_async_copy(vs_hbm.at[rows], vs.at[rows], in_sem.at[1, c]),
            pltpu.make_async_copy(vc_hbm.at[rows], vc.at[rows], in_sem.at[2, c]),
            pltpu.make_async_copy(nu_hbm.at[rows], nu.at[rows], in_sem.at[3, c]),
        ]
        if second:
            todo.append(
                pltpu.make_async_copy(flow_hbm.at[some, rows], before.at[:, rows], before_sem.at[c])
            )
        return todo

    halo_copies = [
        pltpu.make_async_copy(source, target, halo_sem.at[i])
        for i, (source, target) in enumerate(
            zip(halo_hbm, (span_low, span_high, chord_low, chord_high))
        )
    ]
    for copy in halo_copies:
        copy.start()
    for c in range(chunks):
        for copy in copies(c):
            copy.start()

    nothing = jnp.zeros((count, stations, 8, LANES), F32)
    wide[:, 3 : 3 + stations, 0:8, :] = nothing
    wide[:, 3 : 3 + stations, 8 + normal : 16 + normal, :] = nothing
    if profile:
        columns[...] = jnp.zeros(columns.shape, F32)
    for copy in halo_copies:
        copy.wait()
    wide[:, 0:3, 8 : 8 + normal, :] = span_low[some].astype(F32)
    wide[:, 3 + stations : 6 + stations, 8 : 8 + normal, :] = span_high[some].astype(F32)
    place = lax.rem(lax.broadcasted_iota(jnp.int32, (normal, LANES), 1), 8)
    for local, q in enumerate(quantities):
        for half in range(stations // 16):
            near = jnp.where(
                place < 3, chord_low[q, half].astype(F32), chord_high[q, half].astype(F32)
            )
            halos[local, half] = jnp.where(place < 6, near, 0.0)

    def matmuls(p, chord):
        half = lax.div(p, 8)
        parts = []
        for q in range(count):
            for d in range(2):
                slab = wide[q, 3 + 2 * p + d, 8 : 8 + normal, :]
                high = slab.astype(BF16)
                low = (slab - high.astype(F32)).astype(BF16)
                shift = lax.rem(LANES - 8 * lax.rem(2 * p + d, 16), LANES)
                beyond = pltpu.roll(halos[q, half], shift, 1).astype(BF16)
                parts.append(jnp.concatenate([high, low, beyond], axis=1))
        chord[...] = jnp.dot(
            jnp.concatenate(parts), table_ref[...], preferred_element_type=F32
        )

    scale = 0.5 if second else 1.0
    couple = [
        [scale * ((1.0 if q == e else 0.0) + TIME_STEP * mix[q, e]) for e in everything]
        for q in quantities
    ]
    ROWS = 16
    lane = lax.broadcasted_iota(jnp.int32, (ROWS, LANES), 1)

    def body(i, carry):
        pair(2 * i, chord_a, chord_b)
        pair(2 * i + 1, chord_b, chord_a)
        return carry

    def pair(p, chord, later):
        matmuls(jnp.minimum(p + 1, pairs - 1), later)
        for half in range(2):
            s = 2 * p + half
            for tile in range(normal // ROWS):
                rows = slice(ROWS * tile, ROWS * tile + ROWS)
                a = vs[s, rows, :].astype(F32) * (-scale * TIME_STEP / 60)
                b = vc[s, rows, :].astype(F32) * (-scale * TIME_STEP / 60)
                g = nu[s, rows, :].astype(F32) * (scale * TIME_STEP / 180)
                centre = [
                    wide[e - quantities[0], 3 + s, 8 + ROWS * tile : 8 + ROWS * tile + ROWS, :]
                    if e in quantities
                    else state_ref[e, s, rows, :]
                    for e in everything
                ]
                for local, q in enumerate(quantities):

                    def at(ds, dn):
                        low = 8 + ROWS * tile + dn
                        return wide[local, 3 + s + ds, low : low + ROWS, :]

                    first = None
                    both = None
                    for reach in (1, 2, 3):
                        up, down = at(reach, 0), at(-reach, 0)
                        diff = up - down
                        total = (up + down) + (at(0, reach) + at(0, -reach))
                        if FIRST[reach - 1] != 1:
                            diff = diff * float(FIRST[reach - 1])
                        total = total * float(SECOND[reach - 1])
                        first = diff if first is None else first + diff
                        both = total if both is None else both + total
                    start = (2 * local + half) * normal + ROWS * tile
                    crow = slice(start, start + ROWS)
                    chord_first = chord[crow, 0:LANES]
                    chord_second = chord[crow, LANES : 2 * LANES]
                    both = both + (centre[q] * float(2 * CENTRE) + chord_second)
                    value = a * first + b * chord_first + g * both
                    for e in everything:
                        value = value + couple[local][e] * centre[e]
                    if second:
                        value = value + 0.5 * before[local, s, rows, :]
                    result[local, s, rows, :] = value
                    if profile and q == 0:
                        hit = jnp.where(lane == te_ref[s], value, 0.0)
                        column = jnp.sum(hit, axis=1, keepdims=True)
                        columns[rows, :] += jnp.where(lane == s, column, 0.0)
                    if not second:
                        station = lax.rem(s, 16)
                        moved = pltpu.roll(value, lax.rem(3 + 8 * station, LANES), 1)
                        kept = cells[q, lax.div(p, 8), rows, :]
                        cells[q, lax.div(p, 8), rows, :] = jnp.where(
                            lax.div(lane, 8) == station, moved, kept
                        )
        out_copy(p).start()

    def out_copy(p):
        two = pl.ds(2 * p, 2)
        return pltpu.make_async_copy(result.at[:, two], out_hbm.at[some, two], out_sem.at[p])

    def arrive(c):
        for copy in copies(c):
            copy.wait()

    arrive(0)
    matmuls(0, chord_a)
    for c in range(chunks):
        if c + 1 < chunks:
            arrive(c + 1)
        lax.fori_loop(c * pairs // chunks // 2, (c + 1) * pairs // chunks // 2, body, 0)

    if profile:
        amp = fine_dot(columns[...].T, band_ref[...])
        amps[...] = amp[:stations].astype(BF16).astype(F32)
        lane4 = lax.div(lax.broadcasted_iota(jnp.int32, (4, LANES), 1), 16)
        pieces = [jnp.zeros((4, LANES), F32) for _ in range(8)]
        for u in range(8):
            taken = amps[pl.ds(u, 4, stride=8), :]
            for j in range(8):
                shift = (16 * (u - j)) % LANES
                moved = pltpu.roll(taken, shift, 1) if shift else taken
                pieces[j] = jnp.where(lane4 == u, moved, pieces[j])
        for j in range(8):
            amp_out[j] = pieces[j]
    if not second:
        cells_out[...] = cells[...].astype(BF16)
        low_out[...] = result[:, 0:3].astype(BF16)
        high_out[...] = result[:, stations - 3 : stations].astype(BF16)

    def drain(p, carry):
        out_copy(p).wait()
        return carry

    lax.fori_loop(0, pairs, drain, 0)


def section(
    state,
    halos,
    fields,
    mixing,
    table,
    quantities=(0, 1, 2),
    flow=None,
    te_local=None,
    band_table=None,
    onto=None,
):
    total, stations, normal, _ = state.shape
    count = len(quantities)
    second, profile, carried = flow is not None, te_local is not None, onto is not None
    pairs = stations // 2
    hbm = pl.BlockSpec(memory_space=pltpu.HBM)
    vmem = pl.BlockSpec(memory_space=pltpu.VMEM)
    smem = pl.BlockSpec(memory_space=pltpu.SMEM)
    args = [state, *halos, *fields, mixing, table]
    specs = [vmem if second else hbm] + [hbm] * 7 + [smem, vmem]
    shapes = [jax.ShapeDtypeStruct(state.shape, F32)]
    aliases = {}
    if second:
        args.append(flow)
        specs.append(hbm)
    if profile:
        args += [te_local, band_table]
        specs += [smem, vmem]
        shapes.append(jax.ShapeDtypeStruct((8, 4, LANES), F32))
    if carried:
        aliases = {len(args): 0}
        args.append(onto)
        specs.append(hbm)
    if not second:
        shapes += [jax.ShapeDtypeStruct((count, 3, normal, LANES), BF16)] * 2
        shapes.append(jax.ShapeDtypeStruct((count, stations // 16, normal, LANES), BF16))
    args = [
        pltpu.with_memory_space_constraint(x, pltpu.HBM) if spec is hbm else x
        for x, spec in zip(args, specs)
    ]
    field = pltpu.VMEM((stations, normal, LANES), BF16)
    block = pltpu.VMEM((count, stations, normal, LANES), F32)
    differences = pltpu.VMEM((count * 2 * normal, 2 * LANES), F32)
    edge = pltpu.VMEM((count, stations // 16, normal, LANES), F32)
    scratch = [
        pltpu.VMEM((count, stations + 6, normal + 16, LANES), F32),
        block,
        differences,
        differences,
        edge,
        edge,
        field,
        field,
        field,
        pltpu.SemaphoreType.DMA((4, 8)),
        pltpu.SemaphoreType.DMA((pairs,)),
    ]
    if second:
        scratch += [block, pltpu.SemaphoreType.DMA((8,))]
    if profile:
        scratch += [pltpu.VMEM((normal, LANES), F32), pltpu.VMEM((stations, LANES), F32)]
    scratch += [pltpu.VMEM((total, 3, normal, LANES), BF16)] * 2
    scratch += [pltpu.VMEM((total, stations // 16, normal, LANES), BF16)] * 2
    scratch.append(pltpu.SemaphoreType.DMA((4,)))
    return pl.pallas_call(
        functools.partial(
            section_kernel,
            second=second,
            profile=profile,
            carried=carried,
            quantities=quantities,
        ),
        out_shape=tuple(shapes),
        in_specs=specs,
        out_specs=tuple([hbm] + [vmem] * (len(shapes) - 1)),
        scratch_shapes=scratch,
        input_output_aliases=aliases,
        compiler_params=pltpu.CompilerParams(vmem_limit_bytes=20 << 20),
        cost_estimate=pl.CostEstimate(
            flops=20000000 * count, transcendentals=0, bytes_accessed=8000000 * count
        ),
        name=("section_two_" if second else "section_one_") + "".join(map(str, quantities)),
    )(*args)


def spectra_kernel(spectra_ref, wanted_ref, own_ref, send_ref):
    stations, bands, slots = spectra_ref.shape
    width = own_ref.shape[1]
    segs = wanted_ref.shape[0]
    lanes = lax.broadcasted_iota(jnp.int32, (1, width), 1)
    wanted = jnp.zeros((1, width), jnp.int32)
    for k in range(segs):
        wanted = jnp.where(lax.rem(lanes, segs) == k, wanted_ref[k], wanted)
    wanted = wanted + (slots // 2) * lax.rem(lax.div(lanes, segs), 2)
    rows = spectra_ref[...].astype(F32).reshape(stations * bands, slots).astype(BF16)
    slot = lax.broadcasted_iota(jnp.int32, (slots, width), 0)
    choose = jnp.where(slot == wanted, 1.0, 0.0).astype(BF16)
    got = jnp.dot(rows, choose, preferred_element_type=F32)
    row_band = lax.rem(lax.broadcasted_iota(jnp.int32, got.shape, 0), bands)
    lane_band = lax.div(lax.broadcasted_iota(jnp.int32, got.shape, 1), width // bands)
    got = jnp.where(row_band == lane_band, got, 0.0).reshape(stations, bands, width)
    packed = jnp.sum(got, axis=1).astype(BF16)
    own_ref[...] = packed
    for d in range(send_ref.shape[0]):
        send_ref[d] = packed


def stored_kernel(prior_ref, every_ref, own_ref, ramp_ref, out_ref, left):
    bands, stations, tile = prior_ref.shape[1:]
    width = own_ref.shape[1]

    @pl.when(pl.program_id(0) == 0)
    def _():
        own = own_ref[...].astype(F32)
        lane = lax.broadcasted_iota(jnp.int32, own.shape, 1)
        real = lax.rem(lane, 32) < 16
        turned = jnp.where(real, pltpu.roll(own, width - 16, 1), -pltpu.roll(own, 16, 1))
        for c, part in enumerate((own, turned)):
            part = part * ramp_ref[...]
            high = part.astype(BF16).astype(F32)
            low = part - high
            for b in range(bands):
                at = (c * bands + b) * stations
                keep = lax.div(lane, 32) == b
                rows = slice(at, at + stations)
                left[rows, 0:width] = jnp.where(keep, high, 0.0).astype(BF16)
                left[rows, width : 2 * width] = jnp.where(keep, low, 0.0).astype(BF16)

    stored = every_ref[...]
    got = nt_dot(left[...], jnp.concatenate([stored, stored], axis=1))
    out_ref[...] = DECAY * prior_ref[...] + got.reshape(2, bands, stations, tile)


def amplitude_kernel(known_ref, amp_ref, where_ref, rep_ref, out_ref, left):
    step = pl.program_id(0)
    bands, stations, tile = known_ref.shape[1:]
    blocks = tile // stations
    sources = amp_ref.shape[0] // blocks // pl.num_programs(0)

    def spread(source):
        whole = amp_ref[pl.ds(source * sources, sources)].astype(F32)
        total = whole[0]
        for j in range(1, sources):
            total = total + whole[j]
        lane = lax.div(lax.broadcasted_iota(jnp.int32, (8, LANES), 1), 16)
        here = lane == lax.broadcasted_iota(jnp.int32, (8, LANES), 0)
        rows = [
            jnp.where(here, jnp.broadcast_to(total[t : t + 1, :], (8, LANES)), 0.0)
            for t in range(4)
        ]
        return jnp.concatenate(rows).astype(BF16)

    @pl.when(step == 0)
    def _():
        mine = spread(where_ref[0])
        place = lax.rem(lax.broadcasted_iota(jnp.int32, (stations, LANES), 1), 8)
        for c in range(2):
            amp = jnp.dot(mine, rep_ref[c], preferred_element_type=F32)
            for b in range(bands):
                at = (c * bands + b) * stations
                left[at : at + stations, :] = jnp.where(place == b, amp, 0.0).astype(BF16)

    right = jnp.concatenate([spread(step * blocks + i) for i in range(blocks)])
    got = nt_dot(left[...], right)
    out_ref[...] = known_ref[...] + got.reshape(2, bands, stations, tile)


def amplitude_tables():
    index = np.arange(LANES)
    same = (index[:, None] % 16 == index[None, :] % 16).astype(np.float32)
    other = (index[:, None] % 8 == index[None, :] % 8) & (
        (index[:, None] % 16) // 8 != (index[None, :] % 16) // 8
    )
    sign = np.where((index % 16) // 8 == 0, 1.0, -1.0)
    return np.stack([same, other * sign[None, :]]).astype(ml_dtypes.bfloat16)


def shards(
    flow_state,
    vel_span,
    vel_chord,
    viscosity,
    mixing,
    te_index,
    band_response,
    spectra,
    offsets,
    prior_gram_blocks,
):
    count, stations, normal, cells = flow_state.shape
    bands, slots = spectra.shape[1], spectra.shape[2] // 2
    segs = offsets.shape[0]
    span_n, chord_n = lax.axis_size("span"), lax.axis_size("chord")
    span_pos, chord_pos = lax.axis_index("span"), lax.axis_index("chord")
    table = chord_matrices()
    fields = (vel_span, vel_chord, viscosity)

    def exchange(low, high, edge):
        up = [(i, (i + 1) % span_n) for i in range(span_n)]
        down = [(b, a) for a, b in up]
        forward = [(i, i + 1) for i in range(chord_n - 1)]
        backward = [(b, a) for a, b in forward]
        return (
            lax.ppermute(high, "span", up),
            lax.ppermute(low, "span", down),
            lax.ppermute(edge, "chord", forward),
            lax.ppermute(edge, "chord", backward),
        )

    edge_shape = jax.ShapeDtypeStruct((count, stations // 16, normal, LANES), BF16)
    ends_shape = jax.ShapeDtypeStruct((count, 3, normal, LANES), BF16)

    def per_quantity(shape):
        return pl.BlockSpec((1,) + shape.shape[1:], lambda q: (q, 0, 0, 0))

    edge, low, high = pl.pallas_call(
        edges_kernel,
        grid=(count,),
        out_shape=(edge_shape, ends_shape, ends_shape),
        in_specs=[per_quantity(flow_state)],
        out_specs=(per_quantity(edge_shape), per_quantity(ends_shape), per_quantity(ends_shape)),
        name="edges",
    )(flow_state)
    halos = exchange(low, high, edge)

    width = bands * 2 * segs
    _, stored = lax.optimization_barrier((edge, spectra))
    packed, send = pl.pallas_call(
        spectra_kernel,
        out_shape=(
            jax.ShapeDtypeStruct((stations, width), BF16),
            jax.ShapeDtypeStruct((span_n, stations, width), BF16),
        ),
        in_specs=[
            pl.BlockSpec(memory_space=pltpu.VMEM),
            pl.BlockSpec(memory_space=pltpu.SMEM),
        ],
        name="spectra",
    )(stored, offsets)
    halos, send = lax.optimization_barrier((halos, send))
    every = lax.all_to_all(send, "span", 0, 0, tiled=True).reshape(span_n * stations, width)

    (section_one, low, high, edge) = section(flow_state, halos, fields, mixing, table)
    halos = exchange(low, high, edge)

    ramp = np.tile((np.arange(segs, dtype=np.float32) + 1) / segs, 2 * bands)[None]
    tiles = 4
    tile = span_n * stations // tiles
    gram_shape = jax.ShapeDtypeStruct(prior_gram_blocks.shape, F32)
    gram_block = pl.BlockSpec((2, bands, stations, tile), lambda t: (0, 0, 0, t))
    params = pltpu.CompilerParams(vmem_limit_bytes=24 << 20)

    def whole(x):
        return pl.BlockSpec(x.shape, lambda t: (0,) * x.ndim)

    known = pl.pallas_call(
        stored_kernel,
        grid=(tiles,),
        out_shape=gram_shape,
        in_specs=[
            gram_block,
            pl.BlockSpec((tile, width), lambda t: (t, 0)),
            whole(packed),
            whole(ramp),
        ],
        out_specs=gram_block,
        scratch_shapes=[pltpu.VMEM((2 * bands * stations, 2 * width), BF16)],
        compiler_params=params,
        cost_estimate=pl.CostEstimate(
            flops=30000000, transcendentals=0, bytes_accessed=12000000
        ),
        name="gram_stored",
    )(
        pltpu.with_memory_space_constraint(prior_gram_blocks, pltpu.HBM),
        pltpu.with_memory_space_constraint(every, pltpu.HBM),
        packed,
        ramp,
    )
    halos, known = lax.optimization_barrier((halos, known))

    te_local = te_index - chord_pos * cells
    band_table = band_response.reshape(normal, 2, chord_n, bands).transpose(0, 2, 1, 3)
    band_table = band_table.reshape(normal, chord_n * 2 * bands)
    flow_next, amps = section(
        section_one,
        halos,
        fields,
        mixing,
        table,
        (0,),
        flow=flow_state,
        te_local=te_local,
        band_table=band_table,
    )
    amps = jnp.broadcast_to(amps.astype(BF16)[None], (span_n,) + amps.shape)
    amps = lax.all_to_all(
        amps.reshape((span_n * chord_n,) + amps.shape[2:]), ("span", "chord"), 0, 0, tiled=True
    )
    (flow_next,) = section(
        section_one, halos, fields, mixing, table, (1, 2), flow=flow_state, onto=flow_next
    )

    known, flow_next = lax.optimization_barrier((known, flow_next))
    reps = amplitude_tables()
    gram_next = pl.pallas_call(
        amplitude_kernel,
        grid=(tiles,),
        out_shape=gram_shape,
        in_specs=[
            gram_block,
            whole(amps),
            pl.BlockSpec(memory_space=pltpu.SMEM),
            whole(reps),
        ],
        out_specs=gram_block,
        scratch_shapes=[pltpu.VMEM((2 * bands * stations, LANES), BF16)],
        compiler_params=params,
        name="gram_amplitudes",
    )(
        pltpu.with_memory_space_constraint(known, pltpu.HBM),
        amps,
        span_pos.reshape(1),
        reps,
    )
    return (flow_next, gram_next)


def solution(mesh):
    return jax.shard_map(
        shards,
        mesh=mesh,
        in_specs=(
            P(None, "span", None, "chord"),
            P("span", None, "chord"),
            P("span", None, "chord"),
            P("span", None, "chord"),
            P(),
            P("span"),
            P(),
            P("span", "chord", None),
            P(),
            P(None, "chord", "span", None),
        ),
        out_specs=(P(None, "span", None, "chord"), P(None, "chord", "span", None)),
        check_vma=False,
    )
```

```python
import functools

import jax
import jax.numpy as jnp
import ml_dtypes
import numpy as np
from jax import lax
from jax.experimental import pallas as pl
from jax.experimental.pallas import tpu as pltpu
from jax.sharding import PartitionSpec as P

FIRST = (45, -9, 1)
SECOND = (270, -27, 2)
CENTRE = -490
TIME_STEP = 0.6
DECAY = 0.9
F32 = jnp.float32
BF16 = jnp.bfloat16
LANES = 128


def chord_matrices():
    inner = np.zeros((LANES, 2 * LANES), np.float32)
    outer = np.zeros((LANES, 2 * LANES), np.float32)

    def row(cell):
        if cell < 0:
            return outer, cell + 3
        if cell >= LANES:
            return outer, cell - LANES + 3
        return inner, cell

    for cell in range(LANES):
        inner[cell, LANES + cell] += CENTRE
        for reach in (1, 2, 3):
            for sign in (1, -1):
                table, index = row(cell + sign * reach)
                table[index, cell] += sign * FIRST[reach - 1]
                table[index, LANES + cell] += SECOND[reach - 1]
    return np.concatenate([inner, inner, outer]).astype(ml_dtypes.bfloat16)


def nt_dot(a, b):
    return lax.dot_general(a, b, (((1,), (1,)), ((), ())), preferred_element_type=F32)


def fine_dot(a, b):
    def pieces(x):
        one = x.astype(BF16)
        x = x - one.astype(F32)
        two = x.astype(BF16)
        return one, two, (x - two.astype(F32)).astype(BF16)

    left, right = pieces(a), pieces(b)
    total = None
    for i, j in ((2, 0), (0, 2), (1, 1), (1, 0), (0, 1), (0, 0)):
        part = jnp.dot(left[i], right[j], preferred_element_type=F32)
        total = part if total is None else total + part
    return total


def edge_lanes(shape):
    return lax.div(lax.broadcasted_iota(jnp.int32, shape, len(shape) - 1), 8)


def ends_kernel(first_ref, last_ref, low_ref, high_ref):
    low_ref[0] = first_ref[0, 0:3].astype(BF16)
    high_ref[0] = last_ref[0, 1:4].astype(BF16)


def edges_kernel(flow_ref, cells_ref):
    stations, normal = flow_ref.shape[1:3]
    lane = edge_lanes((16, LANES))
    for half in range(stations // 16):
        for tile in range(normal // 16):
            rows = slice(16 * tile, 16 * tile + 16)
            packed = jnp.zeros((16, LANES), F32)
            for s in range(16):
                moved = pltpu.roll(flow_ref[0, 16 * half + s, rows, :], (3 + 8 * s) % LANES, 1)
                packed = jnp.where(lane == s, moved, packed)
            cells_ref[0, half, rows, :] = packed.astype(BF16)


def section_kernel(*refs, second, profile, carried, quantities):
    refs = list(refs)
    take = refs.pop
    state_ref = take(0)
    halo_hbm = [take(0) for _ in range(4)]
    vs_hbm, vc_hbm, nu_hbm = (take(0) for _ in range(3))
    mix, table_ref = take(0), take(0)
    if second:
        flow_hbm = take(0)
    if profile:
        te_ref, band_ref = take(0), take(0)
    if carried:
        take(0)
    out_hbm = take(0)
    if profile:
        amp_out = take(0)
    if not second:
        low_out, high_out, cells_out = (take(0) for _ in range(3))
    wide, result, chord_a, chord_b, halos, cells, vs, vc, nu, in_sem, out_sem = (take(0) for _ in range(11))
    if second:
        before, before_sem = take(0), take(0)
    if profile:
        columns, amps = take(0), take(0)
    span_low, span_high, chord_low, chord_high, halo_sem = (take(0) for _ in range(5))

    count, stations, normal = len(quantities), vs.shape[0], vs.shape[1]
    everything = range(state_ref.shape[0])
    some = pl.ds(quantities[0], count)
    chunks, pairs = 8, stations // 2
    per = stations // chunks

    def copies(c):
        rows = pl.ds(per * c, per)
        todo = [
            pltpu.make_async_copy(
                state_ref.at[some, rows],
                wide.at[:, pl.ds(3 + per * c, per), pl.ds(8, normal), :],
                in_sem.at[0, c],
            ),
            pltpu.make_async_copy(vs_hbm.at[rows], vs.at[rows], in_sem.at[1, c]),
            pltpu.make_async_copy(vc_hbm.at[rows], vc.at[rows], in_sem.at[2, c]),
            pltpu.make_async_copy(nu_hbm.at[rows], nu.at[rows], in_sem.at[3, c]),
        ]
        if second:
            todo.append(
                pltpu.make_async_copy(flow_hbm.at[some, rows], before.at[:, rows], before_sem.at[c])
            )
        return todo

    halo_copies = [
        pltpu.make_async_copy(source, target, halo_sem.at[i])
        for i, (source, target) in enumerate(
            zip(halo_hbm, (span_low, span_high, chord_low, chord_high))
        )
    ]
    for copy in halo_copies:
        copy.start()
    for c in range(chunks):
        for copy in copies(c):
            copy.start()

    nothing = jnp.zeros((count, stations, 8, LANES), F32)
    wide[:, 3 : 3 + stations, 0:8, :] = nothing
    wide[:, 3 : 3 + stations, 8 + normal : 16 + normal, :] = nothing
    if profile:
        columns[...] = jnp.zeros(columns.shape, F32)
    for copy in halo_copies:
        copy.wait()
    wide[:, 0:3, 8 : 8 + normal, :] = span_low[some].astype(F32)
    wide[:, 3 + stations : 6 + stations, 8 : 8 + normal, :] = span_high[some].astype(F32)
    place = lax.rem(lax.broadcasted_iota(jnp.int32, (normal, LANES), 1), 8)
    for local, q in enumerate(quantities):
        for half in range(stations // 16):
            near = jnp.where(
                place < 3, chord_low[q, half].astype(F32), chord_high[q, half].astype(F32)
            )
            halos[local, half] = jnp.where(place < 6, near, 0.0)

    def matmuls(p, chord):
        half = lax.div(p, 8)
        parts = []
        for q in range(count):
            for d in range(2):
                slab = wide[q, 3 + 2 * p + d, 8 : 8 + normal, :]
                high = slab.astype(BF16)
                low = (slab - high.astype(F32)).astype(BF16)
                shift = lax.rem(LANES - 8 * lax.rem(2 * p + d, 16), LANES)
                beyond = pltpu.roll(halos[q, half], shift, 1).astype(BF16)
                parts.append(jnp.concatenate([high, low, beyond], axis=1))
        chord[...] = jnp.dot(
            jnp.concatenate(parts), table_ref[...], preferred_element_type=F32
        )

    scale = 0.5 if second else 1.0
    couple = [
        [scale * ((1.0 if q == e else 0.0) + TIME_STEP * mix[q, e]) for e in everything]
        for q in quantities
    ]
    ROWS = 16
    lane = lax.broadcasted_iota(jnp.int32, (ROWS, LANES), 1)

    def body(i, carry):
        pair(2 * i, chord_a, chord_b)
        pair(2 * i + 1, chord_b, chord_a)
        return carry

    def pair(p, chord, later):
        matmuls(jnp.minimum(p + 1, pairs - 1), later)
        for half in range(2):
            s = 2 * p + half
            for tile in range(normal // ROWS):
                rows = slice(ROWS * tile, ROWS * tile + ROWS)
                a = vs[s, rows, :].astype(F32) * (-scale * TIME_STEP / 60)
                b = vc[s, rows, :].astype(F32) * (-scale * TIME_STEP / 60)
                g = nu[s, rows, :].astype(F32) * (scale * TIME_STEP / 180)
                centre = [
                    wide[e - quantities[0], 3 + s, 8 + ROWS * tile : 8 + ROWS * tile + ROWS, :]
                    if e in quantities
                    else state_ref[e, s, rows, :]
                    for e in everything
                ]
                for local, q in enumerate(quantities):

                    def at(ds, dn):
                        low = 8 + ROWS * tile + dn
                        return wide[local, 3 + s + ds, low : low + ROWS, :]

                    first = None
                    both = None
                    for reach in (1, 2, 3):
                        up, down = at(reach, 0), at(-reach, 0)
                        diff = up - down
                        total = (up + down) + (at(0, reach) + at(0, -reach))
                        if FIRST[reach - 1] != 1:
                            diff = diff * float(FIRST[reach - 1])
                        total = total * float(SECOND[reach - 1])
                        first = diff if first is None else first + diff
                        both = total if both is None else both + total
                    start = (2 * local + half) * normal + ROWS * tile
                    crow = slice(start, start + ROWS)
                    chord_first = chord[crow, 0:LANES]
                    chord_second = chord[crow, LANES : 2 * LANES]
                    both = both + (centre[q] * float(2 * CENTRE) + chord_second)
                    value = a * first + b * chord_first + g * both
                    for e in everything:
                        value = value + couple[local][e] * centre[e]
                    if second:
                        value = value + 0.5 * before[local, s, rows, :]
                    result[local, s, rows, :] = value
                    if profile and q == 0:
                        hit = jnp.where(lane == te_ref[s], value, 0.0)
                        column = jnp.sum(hit, axis=1, keepdims=True)
                        columns[rows, :] += jnp.where(lane == s, column, 0.0)
                    if not second:
                        station = lax.rem(s, 16)
                        moved = pltpu.roll(value, lax.rem(3 + 8 * station, LANES), 1)
                        kept = cells[q, lax.div(p, 8), rows, :]
                        cells[q, lax.div(p, 8), rows, :] = jnp.where(
                            lax.div(lane, 8) == station, moved, kept
                        )
        out_copy(p).start()

    def out_copy(p):
        two = pl.ds(2 * p, 2)
        return pltpu.make_async_copy(result.at[:, two], out_hbm.at[some, two], out_sem.at[p])

    def arrive(c):
        for copy in copies(c):
            copy.wait()

    arrive(0)
    matmuls(0, chord_a)
    for c in range(chunks):
        if c + 1 < chunks:
            arrive(c + 1)
        lax.fori_loop(c * pairs // chunks // 2, (c + 1) * pairs // chunks // 2, body, 0)

    if profile:
        amp = fine_dot(columns[...].T, band_ref[...])
        amps[...] = amp[:stations].astype(BF16).astype(F32)
        lane4 = lax.div(lax.broadcasted_iota(jnp.int32, (4, LANES), 1), 16)
        pieces = [jnp.zeros((4, LANES), F32) for _ in range(8)]
        for u in range(8):
            taken = amps[pl.ds(u, 4, stride=8), :]
            for j in range(8):
                shift = (16 * (u - j)) % LANES
                moved = pltpu.roll(taken, shift, 1) if shift else taken
                pieces[j] = jnp.where(lane4 == u, moved, pieces[j])
        for j in range(8):
            amp_out[j] = pieces[j]
    if not second:
        cells_out[...] = cells[...].astype(BF16)
        low_out[...] = result[:, 0:3].astype(BF16)
        high_out[...] = result[:, stations - 3 : stations].astype(BF16)

    def drain(p, carry):
        out_copy(p).wait()
        return carry

    lax.fori_loop(0, pairs, drain, 0)


def section(
    state,
    halos,
    fields,
    mixing,
    table,
    quantities=(0, 1, 2),
    flow=None,
    te_local=None,
    band_table=None,
    onto=None,
):
    total, stations, normal, _ = state.shape
    count = len(quantities)
    second, profile, carried = flow is not None, te_local is not None, onto is not None
    pairs = stations // 2
    hbm = pl.BlockSpec(memory_space=pltpu.HBM)
    vmem = pl.BlockSpec(memory_space=pltpu.VMEM)
    smem = pl.BlockSpec(memory_space=pltpu.SMEM)
    args = [state, *halos, *fields, mixing, table]
    specs = [vmem if second else hbm] + [hbm] * 7 + [smem, vmem]
    shapes = [jax.ShapeDtypeStruct(state.shape, F32)]
    aliases = {}
    if second:
        args.append(flow)
        specs.append(hbm)
    if profile:
        args += [te_local, band_table]
        specs += [smem, vmem]
        shapes.append(jax.ShapeDtypeStruct((8, 4, LANES), F32))
    if carried:
        aliases = {len(args): 0}
        args.append(onto)
        specs.append(hbm)
    if not second:
        shapes += [jax.ShapeDtypeStruct((count, 3, normal, LANES), BF16)] * 2
        shapes.append(jax.ShapeDtypeStruct((count, stations // 16, normal, LANES), BF16))
    args = [
        pltpu.with_memory_space_constraint(x, pltpu.HBM) if spec is hbm else x
        for x, spec in zip(args, specs)
    ]
    field = pltpu.VMEM((stations, normal, LANES), BF16)
    block = pltpu.VMEM((count, stations, normal, LANES), F32)
    differences = pltpu.VMEM((count * 2 * normal, 2 * LANES), F32)
    edge = pltpu.VMEM((count, stations // 16, normal, LANES), F32)
    scratch = [
        pltpu.VMEM((count, stations + 6, normal + 16, LANES), F32),
        block,
        differences,
        differences,
        edge,
        edge,
        field,
        field,
        field,
        pltpu.SemaphoreType.DMA((4, 8)),
        pltpu.SemaphoreType.DMA((pairs,)),
    ]
    if second:
        scratch += [block, pltpu.SemaphoreType.DMA((8,))]
    if profile:
        scratch += [pltpu.VMEM((normal, LANES), F32), pltpu.VMEM((stations, LANES), F32)]
    scratch += [pltpu.VMEM((total, 3, normal, LANES), BF16)] * 2
    scratch += [pltpu.VMEM((total, stations // 16, normal, LANES), BF16)] * 2
    scratch.append(pltpu.SemaphoreType.DMA((4,)))
    return pl.pallas_call(
        functools.partial(
            section_kernel,
            second=second,
            profile=profile,
            carried=carried,
            quantities=quantities,
        ),
        out_shape=tuple(shapes),
        in_specs=specs,
        out_specs=tuple([hbm] + [vmem] * (len(shapes) - 1)),
        scratch_shapes=scratch,
        input_output_aliases=aliases,
        compiler_params=pltpu.CompilerParams(vmem_limit_bytes=20 << 20),
        cost_estimate=pl.CostEstimate(
            flops=20000000 * count, transcendentals=0, bytes_accessed=8000000 * count
        ),
        name=("section_two_" if second else "section_one_") + "".join(map(str, quantities)),
    )(*args)


def spectra_kernel(spectra_ref, wanted_ref, own_ref, send_ref):
    stations, bands, slots = spectra_ref.shape
    width = own_ref.shape[1]
    segs = wanted_ref.shape[0]
    lanes = lax.broadcasted_iota(jnp.int32, (1, width), 1)
    wanted = jnp.zeros((1, width), jnp.int32)
    for k in range(segs):
        wanted = jnp.where(lax.rem(lanes, segs) == k, wanted_ref[k], wanted)
    wanted = wanted + (slots // 2) * lax.rem(lax.div(lanes, segs), 2)
    rows = spectra_ref[...].astype(F32).reshape(stations * bands, slots).astype(BF16)
    slot = lax.broadcasted_iota(jnp.int32, (slots, width), 0)
    choose = jnp.where(slot == wanted, 1.0, 0.0).astype(BF16)
    got = jnp.dot(rows, choose, preferred_element_type=F32)
    row_band = lax.rem(lax.broadcasted_iota(jnp.int32, got.shape, 0), bands)
    lane_band = lax.div(lax.broadcasted_iota(jnp.int32, got.shape, 1), width // bands)
    got = jnp.where(row_band == lane_band, got, 0.0).reshape(stations, bands, width)
    packed = jnp.sum(got, axis=1).astype(BF16)
    own_ref[...] = packed
    for d in range(send_ref.shape[0]):
        send_ref[d] = packed


def stored_kernel(prior_ref, every_ref, own_ref, ramp_ref, out_ref, left):
    bands, stations, tile = prior_ref.shape[1:]
    width = own_ref.shape[1]

    @pl.when(pl.program_id(0) == 0)
    def _():
        own = own_ref[...].astype(F32)
        lane = lax.broadcasted_iota(jnp.int32, own.shape, 1)
        real = lax.rem(lane, 32) < 16
        turned = jnp.where(real, pltpu.roll(own, width - 16, 1), -pltpu.roll(own, 16, 1))
        for c, part in enumerate((own, turned)):
            part = part * ramp_ref[...]
            high = part.astype(BF16).astype(F32)
            low = part - high
            for b in range(bands):
                at = (c * bands + b) * stations
                keep = lax.div(lane, 32) == b
                rows = slice(at, at + stations)
                left[rows, 0:width] = jnp.where(keep, high, 0.0).astype(BF16)
                left[rows, width : 2 * width] = jnp.where(keep, low, 0.0).astype(BF16)

    stored = every_ref[...]
    got = nt_dot(left[...], jnp.concatenate([stored, stored], axis=1))
    out_ref[...] = DECAY * prior_ref[...] + got.reshape(2, bands, stations, tile)


def amplitude_kernel(known_ref, amp_ref, where_ref, rep_ref, out_ref, left):
    step = pl.program_id(0)
    bands, stations, tile = known_ref.shape[1:]
    blocks = tile // stations
    sources = amp_ref.shape[0] // blocks // pl.num_programs(0)

    def spread(source):
        whole = amp_ref[pl.ds(source * sources, sources)].astype(F32)
        total = whole[0]
        for j in range(1, sources):
            total = total + whole[j]
        lane = lax.div(lax.broadcasted_iota(jnp.int32, (8, LANES), 1), 16)
        here = lane == lax.broadcasted_iota(jnp.int32, (8, LANES), 0)
        rows = [
            jnp.where(here, jnp.broadcast_to(total[t : t + 1, :], (8, LANES)), 0.0)
            for t in range(4)
        ]
        return jnp.concatenate(rows).astype(BF16)

    @pl.when(step == 0)
    def _():
        mine = spread(where_ref[0])
        place = lax.rem(lax.broadcasted_iota(jnp.int32, (stations, LANES), 1), 8)
        for c in range(2):
            amp = jnp.dot(mine, rep_ref[c], preferred_element_type=F32)
            for b in range(bands):
                at = (c * bands + b) * stations
                left[at : at + stations, :] = jnp.where(place == b, amp, 0.0).astype(BF16)

    right = jnp.concatenate([spread(step * blocks + i) for i in range(blocks)])
    got = nt_dot(left[...], right)
    out_ref[...] = known_ref[...] + got.reshape(2, bands, stations, tile)


def amplitude_tables():
    index = np.arange(LANES)
    same = (index[:, None] % 16 == index[None, :] % 16).astype(np.float32)
    other = (index[:, None] % 8 == index[None, :] % 8) & (
        (index[:, None] % 16) // 8 != (index[None, :] % 16) // 8
    )
    sign = np.where((index % 16) // 8 == 0, 1.0, -1.0)
    return np.stack([same, other * sign[None, :]]).astype(ml_dtypes.bfloat16)


def shards(
    flow_state,
    vel_span,
    vel_chord,
    viscosity,
    mixing,
    te_index,
    band_response,
    spectra,
    offsets,
    prior_gram_blocks,
):
    count, stations, normal, cells = flow_state.shape
    bands, slots = spectra.shape[1], spectra.shape[2] // 2
    segs = offsets.shape[0]
    span_n, chord_n = lax.axis_size("span"), lax.axis_size("chord")
    span_pos, chord_pos = lax.axis_index("span"), lax.axis_index("chord")
    table = chord_matrices()
    fields = (vel_span, vel_chord, viscosity)

    def exchange(low, high, edge):
        up = [(i, (i + 1) % span_n) for i in range(span_n)]
        down = [(b, a) for a, b in up]
        forward = [(i, i + 1) for i in range(chord_n - 1)]
        backward = [(b, a) for a, b in forward]
        return (
            lax.ppermute(high, "span", up),
            lax.ppermute(low, "span", down),
            lax.ppermute(edge, "chord", forward),
            lax.ppermute(edge, "chord", backward),
        )

    edge_shape = jax.ShapeDtypeStruct((count, stations // 16, normal, LANES), BF16)
    ends_shape = jax.ShapeDtypeStruct((count, 3, normal, LANES), BF16)

    def per_quantity(shape):
        return pl.BlockSpec((1,) + shape.shape[1:], lambda q: (q, 0, 0, 0))

    four = (1, 4, normal, cells)
    low, high = pl.pallas_call(
        ends_kernel,
        grid=(count,),
        out_shape=(ends_shape, ends_shape),
        in_specs=[
            pl.BlockSpec(four, lambda q: (q, 0, 0, 0)),
            pl.BlockSpec(four, lambda q: (q, stations // 4 - 1, 0, 0)),
        ],
        out_specs=(per_quantity(ends_shape), per_quantity(ends_shape)),
        name="ends",
    )(flow_state, flow_state)
    flow_edges, _ = lax.optimization_barrier((flow_state, low))
    edge = pl.pallas_call(
        edges_kernel,
        grid=(count,),
        out_shape=edge_shape,
        in_specs=[per_quantity(flow_state)],
        out_specs=per_quantity(edge_shape),
        name="edges",
        cost_estimate=pl.CostEstimate(
            flops=10000000, transcendentals=0, bytes_accessed=12000000
        ),
    )(flow_edges)
    halos = exchange(low, high, edge)

    width = bands * 2 * segs
    _, stored = lax.optimization_barrier((edge, spectra))
    packed, send = pl.pallas_call(
        spectra_kernel,
        out_shape=(
            jax.ShapeDtypeStruct((stations, width), BF16),
            jax.ShapeDtypeStruct((span_n, stations, width), BF16),
        ),
        in_specs=[
            pl.BlockSpec(memory_space=pltpu.VMEM),
            pl.BlockSpec(memory_space=pltpu.SMEM),
        ],
        name="spectra",
    )(stored, offsets)
    halos, send = lax.optimization_barrier((halos, send))
    every = lax.all_to_all(send, "span", 0, 0, tiled=True).reshape(span_n * stations, width)

    (section_one, low, high, edge) = section(flow_state, halos, fields, mixing, table)
    ramp = np.tile((np.arange(segs, dtype=np.float32) + 1) / segs, 2 * bands)[None]
    tiles = 4
    tile = span_n * stations // tiles
    gram_shape = jax.ShapeDtypeStruct(prior_gram_blocks.shape, F32)
    gram_block = pl.BlockSpec((2, bands, stations, tile), lambda t: (0, 0, 0, t))
    params = pltpu.CompilerParams(vmem_limit_bytes=24 << 20)

    def whole(x):
        return pl.BlockSpec(x.shape, lambda t: (0,) * x.ndim)

    known = pl.pallas_call(
        stored_kernel,
        grid=(tiles,),
        out_shape=pltpu.HBM(prior_gram_blocks.shape, F32),
        in_specs=[
            gram_block,
            pl.BlockSpec((tile, width), lambda t: (t, 0)),
            whole(packed),
            whole(ramp),
        ],
        out_specs=gram_block,
        scratch_shapes=[pltpu.VMEM((2 * bands * stations, 2 * width), BF16)],
        compiler_params=params,
        cost_estimate=pl.CostEstimate(
            flops=30000000, transcendentals=0, bytes_accessed=12000000
        ),
        name="gram_stored",
    )(
        pltpu.with_memory_space_constraint(prior_gram_blocks, pltpu.HBM),
        pltpu.with_memory_space_constraint(every, pltpu.HBM),
        packed,
        ramp,
    )
    edge, known = lax.optimization_barrier((edge, known))
    halos = exchange(low, high, edge)


    te_local = te_index - chord_pos * cells
    band_table = band_response.reshape(normal, 2, chord_n, bands).transpose(0, 2, 1, 3)
    band_table = band_table.reshape(normal, chord_n * 2 * bands)
    flow_next, amps = section(
        section_one,
        halos,
        fields,
        mixing,
        table,
        (0,),
        flow=flow_state,
        te_local=te_local,
        band_table=band_table,
    )
    amps = jnp.broadcast_to(amps.astype(BF16)[None], (span_n,) + amps.shape)
    amps = lax.all_to_all(
        amps.reshape((span_n * chord_n,) + amps.shape[2:]), ("span", "chord"), 0, 0, tiled=True
    )
    (flow_next,) = section(
        section_one, halos, fields, mixing, table, (1, 2), flow=flow_state, onto=flow_next
    )

    known, flow_next = lax.optimization_barrier((known, flow_next))
    reps = amplitude_tables()
    gram_next = pl.pallas_call(
        amplitude_kernel,
        grid=(tiles,),
        out_shape=gram_shape,
        in_specs=[
            gram_block,
            whole(amps),
            pl.BlockSpec(memory_space=pltpu.SMEM),
            whole(reps),
        ],
        out_specs=gram_block,
        scratch_shapes=[pltpu.VMEM((2 * bands * stations, LANES), BF16)],
        compiler_params=params,
        name="gram_amplitudes",
    )(
        pltpu.with_memory_space_constraint(known, pltpu.HBM),
        amps,
        span_pos.reshape(1),
        reps,
    )
    return (flow_next, gram_next)


def solution(mesh):
    return jax.shard_map(
        shards,
        mesh=mesh,
        in_specs=(
            P(None, "span", None, "chord"),
            P("span", None, "chord"),
            P("span", None, "chord"),
            P("span", None, "chord"),
            P(),
            P("span"),
            P(),
            P("span", "chord", None),
            P(),
            P(None, "chord", "span", None),
        ),
        out_specs=(P(None, "span", None, "chord"), P(None, "chord", "span", None)),
        check_vma=False,
    )
```

```python
import functools

import jax
import jax.numpy as jnp
import ml_dtypes
import numpy as np
from jax import lax
from jax.experimental import pallas as pl
from jax.experimental.pallas import tpu as pltpu
from jax.sharding import PartitionSpec as P

FIRST = (45, -9, 1)
SECOND = (270, -27, 2)
CENTRE = -490
TIME_STEP = 0.6
DECAY = 0.9
F32 = jnp.float32
BF16 = jnp.bfloat16
LANES = 128


def chord_matrices():
    inner = np.zeros((LANES, 2 * LANES), np.float32)
    outer = np.zeros((LANES, 2 * LANES), np.float32)

    def row(cell):
        if cell < 0:
            return outer, cell + 3
        if cell >= LANES:
            return outer, cell - LANES + 3
        return inner, cell

    for cell in range(LANES):
        inner[cell, LANES + cell] += CENTRE
        for reach in (1, 2, 3):
            for sign in (1, -1):
                table, index = row(cell + sign * reach)
                table[index, cell] += sign * FIRST[reach - 1]
                table[index, LANES + cell] += SECOND[reach - 1]
    return np.concatenate([inner, inner, outer]).astype(ml_dtypes.bfloat16)


def nt_dot(a, b):
    return lax.dot_general(a, b, (((1,), (1,)), ((), ())), preferred_element_type=F32)


def fine_dot(a, b):
    def pieces(x):
        one = x.astype(BF16)
        x = x - one.astype(F32)
        two = x.astype(BF16)
        return one, two, (x - two.astype(F32)).astype(BF16)

    left, right = pieces(a), pieces(b)
    total = None
    for i, j in ((2, 0), (0, 2), (1, 1), (1, 0), (0, 1), (0, 0)):
        part = jnp.dot(left[i], right[j], preferred_element_type=F32)
        total = part if total is None else total + part
    return total


def edge_lanes(shape):
    return lax.div(lax.broadcasted_iota(jnp.int32, shape, len(shape) - 1), 8)


def edges_kernel(flow_ref, cells_ref, low_ref, high_ref):
    stations, normal = flow_ref.shape[1:3]
    lane = edge_lanes((16, LANES))
    for half in range(stations // 16):
        for tile in range(normal // 16):
            rows = slice(16 * tile, 16 * tile + 16)
            packed = jnp.zeros((16, LANES), F32)
            for s in range(16):
                moved = pltpu.roll(flow_ref[0, 16 * half + s, rows, :], (3 + 8 * s) % LANES, 1)
                packed = jnp.where(lane == s, moved, packed)
            cells_ref[0, half, rows, :] = packed.astype(BF16)
    low_ref[0] = flow_ref[0, 0:3].astype(BF16)
    high_ref[0] = flow_ref[0, stations - 3 : stations].astype(BF16)


def section_kernel(*refs, second, profile, carried, quantities):
    refs = list(refs)
    take = refs.pop
    state_ref = take(0)
    halo_hbm = [take(0) for _ in range(4)]
    vs_hbm, vc_hbm, nu_hbm = (take(0) for _ in range(3))
    mix, table_ref = take(0), take(0)
    if second:
        flow_hbm = take(0)
    if profile:
        te_ref, band_ref = take(0), take(0)
    if carried:
        take(0)
    out_hbm = take(0)
    if profile:
        amp_out = take(0)
    if not second:
        low_out, high_out, cells_out = (take(0) for _ in range(3))
    wide, result, chord_a, chord_b, halos, cells, vs, vc, nu, in_sem, out_sem = (take(0) for _ in range(11))
    if second:
        before, before_sem = take(0), take(0)
    if profile:
        columns, amps = take(0), take(0)
    span_low, span_high, chord_low, chord_high, halo_sem = (take(0) for _ in range(5))

    count, stations, normal = len(quantities), vs.shape[0], vs.shape[1]
    everything = range(state_ref.shape[0])
    some = pl.ds(quantities[0], count)
    chunks, pairs = 8, stations // 2
    per = stations // chunks

    def copies(c):
        rows = pl.ds(per * c, per)
        todo = [
            pltpu.make_async_copy(
                state_ref.at[some, rows],
                wide.at[:, pl.ds(3 + per * c, per), pl.ds(8, normal), :],
                in_sem.at[0, c],
            ),
            pltpu.make_async_copy(vs_hbm.at[rows], vs.at[rows], in_sem.at[1, c]),
            pltpu.make_async_copy(vc_hbm.at[rows], vc.at[rows], in_sem.at[2, c]),
            pltpu.make_async_copy(nu_hbm.at[rows], nu.at[rows], in_sem.at[3, c]),
        ]
        if second:
            todo.append(
                pltpu.make_async_copy(flow_hbm.at[some, rows], before.at[:, rows], before_sem.at[c])
            )
        return todo

    halo_copies = [
        pltpu.make_async_copy(source, target, halo_sem.at[i])
        for i, (source, target) in enumerate(
            zip(halo_hbm, (span_low, span_high, chord_low, chord_high))
        )
    ]
    for copy in halo_copies:
        copy.start()
    for c in range(chunks):
        for copy in copies(c):
            copy.start()

    nothing = jnp.zeros((count, stations, 8, LANES), F32)
    wide[:, 3 : 3 + stations, 0:8, :] = nothing
    wide[:, 3 : 3 + stations, 8 + normal : 16 + normal, :] = nothing
    if profile:
        columns[...] = jnp.zeros(columns.shape, F32)
    for copy in halo_copies:
        copy.wait()
    wide[:, 0:3, 8 : 8 + normal, :] = span_low[some].astype(F32)
    wide[:, 3 + stations : 6 + stations, 8 : 8 + normal, :] = span_high[some].astype(F32)
    place = lax.rem(lax.broadcasted_iota(jnp.int32, (normal, LANES), 1), 8)
    for local, q in enumerate(quantities):
        for half in range(stations // 16):
            near = jnp.where(
                place < 3, chord_low[q, half].astype(F32), chord_high[q, half].astype(F32)
            )
            halos[local, half] = jnp.where(place < 6, near, 0.0)

    def matmuls(p, chord):
        half = lax.div(p, 8)
        parts = []
        for q in range(count):
            for d in range(2):
                slab = wide[q, 3 + 2 * p + d, 8 : 8 + normal, :]
                high = slab.astype(BF16)
                low = (slab - high.astype(F32)).astype(BF16)
                shift = lax.rem(LANES - 8 * lax.rem(2 * p + d, 16), LANES)
                beyond = pltpu.roll(halos[q, half], shift, 1).astype(BF16)
                parts.append(jnp.concatenate([high, low, beyond], axis=1))
        chord[...] = jnp.dot(
            jnp.concatenate(parts), table_ref[...], preferred_element_type=F32
        )

    scale = 0.5 if second else 1.0
    couple = [
        [scale * ((1.0 if q == e else 0.0) + TIME_STEP * mix[q, e]) for e in everything]
        for q in quantities
    ]
    ROWS = 16
    lane = lax.broadcasted_iota(jnp.int32, (ROWS, LANES), 1)

    def body(i, carry):
        pair(2 * i, chord_a, chord_b)
        pair(2 * i + 1, chord_b, chord_a)
        return carry

    def pair(p, chord, later):
        matmuls(jnp.minimum(p + 1, pairs - 1), later)
        for half in range(2):
            s = 2 * p + half
            for tile in range(normal // ROWS):
                rows = slice(ROWS * tile, ROWS * tile + ROWS)
                a = vs[s, rows, :].astype(F32) * (-scale * TIME_STEP / 60)
                b = vc[s, rows, :].astype(F32) * (-scale * TIME_STEP / 60)
                g = nu[s, rows, :].astype(F32) * (scale * TIME_STEP / 180)
                centre = [
                    wide[e - quantities[0], 3 + s, 8 + ROWS * tile : 8 + ROWS * tile + ROWS, :]
                    if e in quantities
                    else state_ref[e, s, rows, :]
                    for e in everything
                ]
                for local, q in enumerate(quantities):

                    def at(ds, dn):
                        low = 8 + ROWS * tile + dn
                        return wide[local, 3 + s + ds, low : low + ROWS, :]

                    first = None
                    both = None
                    for reach in (1, 2, 3):
                        up, down = at(reach, 0), at(-reach, 0)
                        diff = up - down
                        total = (up + down) + (at(0, reach) + at(0, -reach))
                        if FIRST[reach - 1] != 1:
                            diff = diff * float(FIRST[reach - 1])
                        total = total * float(SECOND[reach - 1])
                        first = diff if first is None else first + diff
                        both = total if both is None else both + total
                    start = (2 * local + half) * normal + ROWS * tile
                    crow = slice(start, start + ROWS)
                    chord_first = chord[crow, 0:LANES]
                    chord_second = chord[crow, LANES : 2 * LANES]
                    both = both + (centre[q] * float(2 * CENTRE) + chord_second)
                    value = a * first + b * chord_first + g * both
                    for e in everything:
                        value = value + couple[local][e] * centre[e]
                    if second:
                        value = value + 0.5 * before[local, s, rows, :]
                    result[local, s, rows, :] = value
                    if profile and q == 0:
                        hit = jnp.where(lane == te_ref[s], value, 0.0)
                        column = jnp.sum(hit, axis=1, keepdims=True)
                        columns[rows, :] += jnp.where(lane == s, column, 0.0)
                    if not second:
                        station = lax.rem(s, 16)
                        moved = pltpu.roll(value, lax.rem(3 + 8 * station, LANES), 1)
                        kept = cells[q, lax.div(p, 8), rows, :]
                        cells[q, lax.div(p, 8), rows, :] = jnp.where(
                            lax.div(lane, 8) == station, moved, kept
                        )
        out_copy(p).start()

    def out_copy(p):
        two = pl.ds(2 * p, 2)
        return pltpu.make_async_copy(result.at[:, two], out_hbm.at[some, two], out_sem.at[p])

    def arrive(c):
        for copy in copies(c):
            copy.wait()

    arrive(0)
    matmuls(0, chord_a)
    for c in range(chunks):
        if c + 1 < chunks:
            arrive(c + 1)
        lax.fori_loop(c * pairs // chunks // 2, (c + 1) * pairs // chunks // 2, body, 0)

    if profile:
        amp = fine_dot(columns[...].T, band_ref[...])
        amps[...] = amp[:stations].astype(BF16).astype(F32)
        lane4 = lax.div(lax.broadcasted_iota(jnp.int32, (4, LANES), 1), 16)
        pieces = [jnp.zeros((4, LANES), F32) for _ in range(8)]
        for u in range(8):
            taken = amps[pl.ds(u, 4, stride=8), :]
            for j in range(8):
                shift = (16 * (u - j)) % LANES
                moved = pltpu.roll(taken, shift, 1) if shift else taken
                pieces[j] = jnp.where(lane4 == u, moved, pieces[j])
        sent = jnp.stack(pieces).astype(BF16)
        for d in range(amp_out.shape[0]):
            amp_out[d] = sent
    if not second:
        cells_out[...] = cells[...].astype(BF16)
        low_out[...] = result[:, 0:3].astype(BF16)
        high_out[...] = result[:, stations - 3 : stations].astype(BF16)

    def drain(p, carry):
        out_copy(p).wait()
        return carry

    lax.fori_loop(0, pairs, drain, 0)


def section(
    state,
    halos,
    fields,
    mixing,
    table,
    quantities=(0, 1, 2),
    flow=None,
    te_local=None,
    band_table=None,
    onto=None,
    receivers=1,
):
    total, stations, normal, _ = state.shape
    count = len(quantities)
    second, profile, carried = flow is not None, te_local is not None, onto is not None
    pairs = stations // 2
    hbm = pl.BlockSpec(memory_space=pltpu.HBM)
    vmem = pl.BlockSpec(memory_space=pltpu.VMEM)
    smem = pl.BlockSpec(memory_space=pltpu.SMEM)
    args = [state, *halos, *fields, mixing, table]
    specs = [vmem if second else hbm] + [hbm] * 7 + [smem, vmem]
    shapes = [jax.ShapeDtypeStruct(state.shape, F32)]
    aliases = {}
    if second:
        args.append(flow)
        specs.append(hbm)
    if profile:
        args += [te_local, band_table]
        specs += [smem, vmem]
        shapes.append(jax.ShapeDtypeStruct((receivers, 8, 4, LANES), BF16))
    if carried:
        aliases = {len(args): 0}
        args.append(onto)
        specs.append(hbm)
    if not second:
        shapes += [jax.ShapeDtypeStruct((count, 3, normal, LANES), BF16)] * 2
        shapes.append(jax.ShapeDtypeStruct((count, stations // 16, normal, LANES), BF16))
    args = [
        pltpu.with_memory_space_constraint(x, pltpu.HBM) if spec is hbm else x
        for x, spec in zip(args, specs)
    ]
    field = pltpu.VMEM((stations, normal, LANES), BF16)
    block = pltpu.VMEM((count, stations, normal, LANES), F32)
    differences = pltpu.VMEM((count * 2 * normal, 2 * LANES), F32)
    edge = pltpu.VMEM((count, stations // 16, normal, LANES), F32)
    scratch = [
        pltpu.VMEM((count, stations + 6, normal + 16, LANES), F32),
        block,
        differences,
        differences,
        edge,
        edge,
        field,
        field,
        field,
        pltpu.SemaphoreType.DMA((4, 8)),
        pltpu.SemaphoreType.DMA((pairs,)),
    ]
    if second:
        scratch += [block, pltpu.SemaphoreType.DMA((8,))]
    if profile:
        scratch += [pltpu.VMEM((normal, LANES), F32), pltpu.VMEM((stations, LANES), F32)]
    scratch += [pltpu.VMEM((total, 3, normal, LANES), BF16)] * 2
    scratch += [pltpu.VMEM((total, stations // 16, normal, LANES), BF16)] * 2
    scratch.append(pltpu.SemaphoreType.DMA((4,)))
    return pl.pallas_call(
        functools.partial(
            section_kernel,
            second=second,
            profile=profile,
            carried=carried,
            quantities=quantities,
        ),
        out_shape=tuple(shapes),
        in_specs=specs,
        out_specs=tuple([hbm] + [vmem] * (len(shapes) - 1)),
        scratch_shapes=scratch,
        input_output_aliases=aliases,
        compiler_params=pltpu.CompilerParams(vmem_limit_bytes=20 << 20),
        cost_estimate=pl.CostEstimate(
            flops=20000000 * count, transcendentals=0, bytes_accessed=8000000 * count
        ),
        name=("section_two_" if second else "section_one_") + "".join(map(str, quantities)),
    )(*args)


def spectra_kernel(spectra_ref, wanted_ref, own_ref, send_ref):
    stations, bands, slots = spectra_ref.shape
    width = own_ref.shape[1]
    segs = wanted_ref.shape[0]
    lanes = lax.broadcasted_iota(jnp.int32, (1, width), 1)
    wanted = jnp.zeros((1, width), jnp.int32)
    for k in range(segs):
        wanted = jnp.where(lax.rem(lanes, segs) == k, wanted_ref[k], wanted)
    wanted = wanted + (slots // 2) * lax.rem(lax.div(lanes, segs), 2)
    rows = spectra_ref[...].astype(F32).reshape(stations * bands, slots).astype(BF16)
    slot = lax.broadcasted_iota(jnp.int32, (slots, width), 0)
    choose = jnp.where(slot == wanted, 1.0, 0.0).astype(BF16)
    got = jnp.dot(rows, choose, preferred_element_type=F32)
    row_band = lax.rem(lax.broadcasted_iota(jnp.int32, got.shape, 0), bands)
    lane_band = lax.div(lax.broadcasted_iota(jnp.int32, got.shape, 1), width // bands)
    got = jnp.where(row_band == lane_band, got, 0.0).reshape(stations, bands, width)
    packed = jnp.sum(got, axis=1).astype(BF16)
    own_ref[...] = packed
    for d in range(send_ref.shape[0]):
        send_ref[d] = packed


def stored_kernel(prior_ref, every_ref, own_ref, ramp_ref, out_ref, left):
    bands, stations, tile = prior_ref.shape[1:]
    width = own_ref.shape[1]

    @pl.when(pl.program_id(0) == 0)
    def _():
        own = own_ref[...].astype(F32)
        lane = lax.broadcasted_iota(jnp.int32, own.shape, 1)
        real = lax.rem(lane, 32) < 16
        turned = jnp.where(real, pltpu.roll(own, width - 16, 1), -pltpu.roll(own, 16, 1))
        for c, part in enumerate((own, turned)):
            part = part * ramp_ref[...]
            high = part.astype(BF16).astype(F32)
            low = part - high
            for b in range(bands):
                at = (c * bands + b) * stations
                keep = lax.div(lane, 32) == b
                rows = slice(at, at + stations)
                left[rows, 0:width] = jnp.where(keep, high, 0.0).astype(BF16)
                left[rows, width : 2 * width] = jnp.where(keep, low, 0.0).astype(BF16)

    stored = every_ref[...]
    got = nt_dot(left[...], jnp.concatenate([stored, stored], axis=1))
    out_ref[...] = DECAY * prior_ref[...] + got.reshape(2, bands, stations, tile)


def amplitude_kernel(known_ref, amp_ref, where_ref, rep_ref, out_ref, left):
    step = pl.program_id(0)
    bands, stations, tile = known_ref.shape[1:]
    blocks = tile // stations
    sources = amp_ref.shape[0] // blocks // pl.num_programs(0)

    def spread(source):
        whole = amp_ref[pl.ds(source * sources, sources)].astype(F32)
        total = whole[0]
        for j in range(1, sources):
            total = total + whole[j]
        lane = lax.div(lax.broadcasted_iota(jnp.int32, (8, LANES), 1), 16)
        here = lane == lax.broadcasted_iota(jnp.int32, (8, LANES), 0)
        rows = [
            jnp.where(here, jnp.broadcast_to(total[t : t + 1, :], (8, LANES)), 0.0)
            for t in range(4)
        ]
        return jnp.concatenate(rows).astype(BF16)

    @pl.when(step == 0)
    def _():
        mine = spread(where_ref[0])
        place = lax.rem(lax.broadcasted_iota(jnp.int32, (stations, LANES), 1), 8)
        for c in range(2):
            amp = jnp.dot(mine, rep_ref[c], preferred_element_type=F32)
            for b in range(bands):
                at = (c * bands + b) * stations
                left[at : at + stations, :] = jnp.where(place == b, amp, 0.0).astype(BF16)

    right = jnp.concatenate([spread(step * blocks + i) for i in range(blocks)])
    got = nt_dot(left[...], right)
    out_ref[...] = known_ref[...] + got.reshape(2, bands, stations, tile)


def amplitude_tables():
    index = np.arange(LANES)
    same = (index[:, None] % 16 == index[None, :] % 16).astype(np.float32)
    other = (index[:, None] % 8 == index[None, :] % 8) & (
        (index[:, None] % 16) // 8 != (index[None, :] % 16) // 8
    )
    sign = np.where((index % 16) // 8 == 0, 1.0, -1.0)
    return np.stack([same, other * sign[None, :]]).astype(ml_dtypes.bfloat16)


def shards(
    flow_state,
    vel_span,
    vel_chord,
    viscosity,
    mixing,
    te_index,
    band_response,
    spectra,
    offsets,
    prior_gram_blocks,
):
    count, stations, normal, cells = flow_state.shape
    bands, slots = spectra.shape[1], spectra.shape[2] // 2
    segs = offsets.shape[0]
    span_n, chord_n = lax.axis_size("span"), lax.axis_size("chord")
    span_pos, chord_pos = lax.axis_index("span"), lax.axis_index("chord")
    table = chord_matrices()
    fields = (vel_span, vel_chord, viscosity)

    def exchange(low, high, edge):
        up = [(i, (i + 1) % span_n) for i in range(span_n)]
        down = [(b, a) for a, b in up]
        forward = [(i, i + 1) for i in range(chord_n - 1)]
        backward = [(b, a) for a, b in forward]
        return (
            lax.ppermute(high, "span", up),
            lax.ppermute(low, "span", down),
            lax.ppermute(edge, "chord", forward),
            lax.ppermute(edge, "chord", backward),
        )

    edge_shape = jax.ShapeDtypeStruct((count, stations // 16, normal, LANES), BF16)
    ends_shape = jax.ShapeDtypeStruct((count, 3, normal, LANES), BF16)

    def per_quantity(shape):
        return pl.BlockSpec((1,) + shape.shape[1:], lambda q: (q, 0, 0, 0))

    edge, low, high = pl.pallas_call(
        edges_kernel,
        grid=(count,),
        out_shape=(edge_shape, ends_shape, ends_shape),
        in_specs=[per_quantity(flow_state)],
        out_specs=(per_quantity(edge_shape), per_quantity(ends_shape), per_quantity(ends_shape)),
        name="edges",
    )(flow_state)
    halos = exchange(low, high, edge)

    width = bands * 2 * segs
    _, stored = lax.optimization_barrier((edge, spectra))
    packed, send = pl.pallas_call(
        spectra_kernel,
        out_shape=(
            jax.ShapeDtypeStruct((stations, width), BF16),
            jax.ShapeDtypeStruct((span_n, stations, width), BF16),
        ),
        in_specs=[
            pl.BlockSpec(memory_space=pltpu.VMEM),
            pl.BlockSpec(memory_space=pltpu.SMEM),
        ],
        name="spectra",
    )(stored, offsets)
    halos, send = lax.optimization_barrier((halos, send))
    every = lax.all_to_all(send, "span", 0, 0, tiled=True).reshape(span_n * stations, width)

    (section_one, low, high, edge) = section(flow_state, halos, fields, mixing, table)
    halos = exchange(low, high, edge)

    ramp = np.tile((np.arange(segs, dtype=np.float32) + 1) / segs, 2 * bands)[None]
    tiles = 4
    tile = span_n * stations // tiles
    gram_shape = jax.ShapeDtypeStruct(prior_gram_blocks.shape, F32)
    gram_block = pl.BlockSpec((2, bands, stations, tile), lambda t: (0, 0, 0, t))
    params = pltpu.CompilerParams(vmem_limit_bytes=24 << 20)

    def whole(x):
        return pl.BlockSpec(x.shape, lambda t: (0,) * x.ndim)

    known = pl.pallas_call(
        stored_kernel,
        grid=(tiles,),
        out_shape=gram_shape,
        in_specs=[
            gram_block,
            pl.BlockSpec((tile, width), lambda t: (t, 0)),
            whole(packed),
            whole(ramp),
        ],
        out_specs=gram_block,
        scratch_shapes=[pltpu.VMEM((2 * bands * stations, 2 * width), BF16)],
        compiler_params=params,
        cost_estimate=pl.CostEstimate(
            flops=30000000, transcendentals=0, bytes_accessed=12000000
        ),
        name="gram_stored",
    )(
        pltpu.with_memory_space_constraint(prior_gram_blocks, pltpu.HBM),
        pltpu.with_memory_space_constraint(every, pltpu.HBM),
        packed,
        ramp,
    )
    halos, known = lax.optimization_barrier((halos, known))

    te_local = te_index - chord_pos * cells
    band_table = band_response.reshape(normal, 2, chord_n, bands).transpose(0, 2, 1, 3)
    band_table = band_table.reshape(normal, chord_n * 2 * bands)
    flow_next, amps = section(
        section_one,
        halos,
        fields,
        mixing,
        table,
        (0,),
        flow=flow_state,
        te_local=te_local,
        band_table=band_table,
        receivers=span_n,
    )
    amps = lax.all_to_all(
        amps.reshape((span_n * chord_n,) + amps.shape[2:]), ("span", "chord"), 0, 0, tiled=True
    )
    (flow_next,) = section(
        section_one, halos, fields, mixing, table, (1, 2), flow=flow_state, onto=flow_next
    )

    known, flow_next = lax.optimization_barrier((known, flow_next))
    reps = amplitude_tables()
    gram_next = pl.pallas_call(
        amplitude_kernel,
        grid=(tiles,),
        out_shape=gram_shape,
        in_specs=[
            gram_block,
            whole(amps),
            pl.BlockSpec(memory_space=pltpu.SMEM),
            whole(reps),
        ],
        out_specs=gram_block,
        scratch_shapes=[pltpu.VMEM((2 * bands * stations, LANES), BF16)],
        compiler_params=params,
        name="gram_amplitudes",
    )(
        pltpu.with_memory_space_constraint(known, pltpu.HBM),
        amps,
        span_pos.reshape(1),
        reps,
    )
    return (flow_next, gram_next)


def solution(mesh):
    return jax.shard_map(
        shards,
        mesh=mesh,
        in_specs=(
            P(None, "span", None, "chord"),
            P("span", None, "chord"),
            P("span", None, "chord"),
            P("span", None, "chord"),
            P(),
            P("span"),
            P(),
            P("span", "chord", None),
            P(),
            P(None, "chord", "span", None),
        ),
        out_specs=(P(None, "span", None, "chord"), P(None, "chord", "span", None)),
        check_vma=False,
    )
```
